512 devices in a mesh: probe: 8 (over y_lo, x), slab: 64 (over y_hi, z, core).
Axes of the slice: x: 4, y: 4 (y_hi: 2, y_lo: 2; y = y_hi * 2 + y_lo), z: 16, core: 2. Of those that a mesh axis runs over, the one named last changes fastest.
Arguments:
- probes: float32 [3, 512, 65536], P(None, 'probe', 'slab'), may hold values from -6 to 6
- viscosity: float32 [65536], P('slab'), may hold values from 0.8 to 1.25
- coupling: float32 [4, 3, 3, 65536], P(None, None, None, 'slab'), may hold values from -0.06 to 0.06
- misfit_weight: float32 [3, 65536], P(None, 'slab'), may hold values from 0.7 to 1.4
- band_offsets: int32 [4], replicated, may hold values from -4 to 4, as said below
Outputs:
- basis: float32 [3, 512, 65536], P(None, 'probe', 'slab')
- r_factor: float32 [512, 512], P('probe')
The draws below stay inside these ranges and needn't reach their ends.
Inputs may be any that keep to these rules, and one draw needn't show every extreme that they name: `band_offsets`: 4 distinct nonzero offsets; both -4 and 4 are among them.
All inputs are finite; a program needn't handle non-finite values.
Results may differ from the reference program's by a relative error of at most 0.0003.
Values sent between devices are 32-bit elements; how exact they have to be, the bound alone decides.
A program may use at most 64 MiB of HBM per device.

```python
import math
import jax
import jax.numpy as jnp
from jax import lax

PROBES = 512
REACH = 4
BANDS = 4
CELLS = 65536
ROWS = 196608


def draw_band_offsets(key, part):
    first_key, second_key = jax.random.split(key)
    candidates = jnp.concatenate([jnp.arange(1 - REACH, 0), jnp.arange(1, REACH)]).astype(jnp.int32)
    picked = jax.random.permutation(first_key, candidates)[:2]
    ends = jnp.array([0 - REACH, REACH], dtype=jnp.int32)
    return jax.random.permutation(second_key, jnp.concatenate([ends, picked]))


def level_of(rng, extent, cuts, smallest, largest):
    def one(position, shards_of):
        draws = jax.random.uniform(jax.random.fold_in(jax.random.fold_in(rng, 6), position), (shards_of,), jnp.float32, smallest / len(cuts), largest / len(cuts))
        return jnp.repeat(jnp.exp(draws), extent[position] // shards_of).reshape((-1,) + (1,) * (len(extent) - position - 1))

    factor_of = one(*cuts[0])
    for cut in cuts[1:]:
        factor_of = factor_of * one(*cut)
    return factor_of


def normal_values(key, dims, deviation, reach, pieces=(), kind=jnp.bfloat16):
    gain = level_of(key, dims, pieces, -0.22, 0.18) if pieces else 1.0
    values = jax.random.normal(key, dims, jnp.float32) * deviation * gain
    return jnp.minimum(jnp.maximum(values, -reach), reach).astype(kind)


def setup_inputs(seed: int = 0) -> dict:
    arg_keys = jax.random.split(jax.random.key(seed), 6)
    probes = normal_values(arg_keys[0], (3, PROBES, CELLS), 1.0, 6.0, ((1, 8), (2, 64)), jnp.float32)
    viscosity = jnp.clip(jnp.exp(math.log(1.25) - 0.4462871 * jax.random.uniform(arg_keys[1], (CELLS,), jnp.float32) ** level_of(arg_keys[1], (CELLS,), ((0, 64),), -0.2, 0.2)), 0.8, 1.25)
    coupling = jnp.clip(jax.random.uniform(arg_keys[2], (BANDS, 3, 3, CELLS), jnp.float32, -0.06, 0.06) * level_of(arg_keys[2], (BANDS, 3, 3, CELLS), ((3, 64),), -0.4, 0.0), -0.06, 0.06)
    misfit_weight = jnp.clip(jnp.exp(math.log(1.4) - 0.6931472 * jax.random.uniform(arg_keys[3], (3, CELLS), jnp.float32) ** level_of(arg_keys[3], (3, CELLS), ((1, 64),), -0.2, 0.2)), 0.7, 1.4)
    band_offsets = draw_band_offsets(jax.random.fold_in(arg_keys[5], 71), 0)
    return dict(probes=probes, viscosity=viscosity, coupling=coupling, misfit_weight=misfit_weight, band_offsets=band_offsets)


def small_cholesky(matrix):
    size = matrix.shape[0]
    places = jnp.arange(size, dtype=jnp.int32)

    def column_step(index, lower):
        row_j = lax.dynamic_index_in_dim(lower, index, 0, keepdims=False)
        col_a = lax.dynamic_index_in_dim(matrix, index, 1, keepdims=False)
        column = col_a - jnp.dot(lower, row_j, precision=lax.Precision.HIGHEST)
        pivot = jnp.sqrt(jnp.sum(jnp.where(places == index, column, 0.0)))
        filled = jnp.where(places > index, column / pivot, jnp.where(places == index, pivot, 0.0))
        marker = (places == index).astype(matrix.dtype)
        return lower + filled[:, None] * marker[None, :]
    return lax.fori_loop(0, size, column_step, jnp.zeros_like(matrix))

def small_lower_inverse(lower):
    size = lower.shape[0]
    places = jnp.arange(size, dtype=jnp.int32)

    def row_step(index, inverse):
        row_l = lax.dynamic_index_in_dim(lower, index, 0, keepdims=False)
        diag_value = jnp.sum(jnp.where(places == index, row_l, 0.0))
        marker = (places == index).astype(lower.dtype)
        strict = jnp.where(places < index, row_l, 0.0)
        new_row = (marker - jnp.dot(strict, inverse, precision=lax.Precision.HIGHEST)) / diag_value
        return inverse + marker[:, None] * new_row[None, :]
    return lax.fori_loop(0, size, row_step, jnp.zeros_like(lower))

def factorize(gram):
    size = gram.shape[0]
    width = 64
    count = size // width
    work = gram
    lower_blocks = {}
    inverse_diag = []
    for outer in range(count):
        lo = outer * width
        diag_block = work[lo:lo + width, lo:lo + width]
        diag_lower = small_cholesky(diag_block)
        diag_inverse = small_lower_inverse(diag_lower)
        lower_blocks[outer, outer] = diag_lower
        inverse_diag.append(diag_inverse)
        if outer + 1 < count:
            below = jnp.dot(work[lo + width:, lo:lo + width], diag_inverse.T, precision=lax.Precision.HIGHEST)
            for inner in range(outer + 1, count):
                start = (inner - outer - 1) * width
                lower_blocks[inner, outer] = below[start:start + width]
            trailing = work[lo + width:, lo + width:] - jnp.dot(below, below.T, precision=lax.Precision.HIGHEST)
            work = work.at[lo + width:, lo + width:].set(trailing)
    zero_block = jnp.zeros((width, width), dtype=gram.dtype)
    lower_rows = []
    for inner in range(count):
        lower_rows.append(jnp.concatenate([lower_blocks.get((inner, outer), zero_block) for outer in range(count)], 1))
    lower = jnp.concatenate(lower_rows, 0)
    inverse_blocks = {}
    for outer in range(count):
        inverse_blocks[outer, outer] = inverse_diag[outer]
        for inner in range(outer + 1, count):
            total = jnp.zeros((width, width), dtype=gram.dtype)
            for middle in range(outer, inner):
                total = total + jnp.dot(lower_blocks[inner, middle], inverse_blocks[middle, outer], precision=lax.Precision.HIGHEST)
            inverse_blocks[inner, outer] = 0.0 - jnp.dot(inverse_diag[inner], total, precision=lax.Precision.HIGHEST)
    inverse_rows = []
    for inner in range(count):
        inverse_rows.append(jnp.concatenate([inverse_blocks.get((inner, outer), zero_block) for outer in range(count)], 1))
    lower_inverse = jnp.concatenate(inverse_rows, 0)
    return (lower.T, lower_inverse.T)

def tangent(values, viscosity, coupling, offsets):
    padded = jnp.pad(values, ((0, 0), (0, 0), (REACH, REACH)))
    summed = [values[0], values[1], values[2]]
    for which_band in range(BANDS):
        start = (REACH + offsets[which_band]).astype(jnp.int32)
        shifted = lax.dynamic_slice_in_dim(padded, start, CELLS, 2)
        for out_comp in range(3):
            for in_comp in range(3):
                summed[out_comp] = summed[out_comp] + coupling[which_band, out_comp, in_comp][None, :] * shifted[in_comp]
    return viscosity[None, None, :] * jnp.stack(summed)

def adjoint(scaled, coupling, offsets):
    result = scaled
    for which_band in range(BANDS):
        parts = []
        for in_comp in range(3):
            acc = coupling[which_band, 0, in_comp][None, :] * scaled[0]
            acc = acc + coupling[which_band, 1, in_comp][None, :] * scaled[1]
            acc = acc + coupling[which_band, 2, in_comp][None, :] * scaled[2]
            parts.append(acc)
        padded = jnp.pad(jnp.stack(parts), ((0, 0), (0, 0), (REACH, REACH)))
        start = (REACH - offsets[which_band]).astype(jnp.int32)
        result = result + lax.dynamic_slice_in_dim(padded, start, CELLS, 2)
    return result

def hessian(values, viscosity, coupling, weight, offsets):
    image = tangent(values, viscosity, coupling, offsets)
    scaled = viscosity[None, None, :] * (weight[:, None, :] * image)
    return adjoint(scaled, coupling, offsets)

def reference(probes, viscosity, coupling, misfit_weight, band_offsets):
    panel = hessian(probes, viscosity, coupling, misfit_weight, band_offsets)
    panel = hessian(panel, viscosity, coupling, misfit_weight, band_offsets)
    gram = jnp.einsum('kpc,kqc->pq', panel, panel, precision=lax.Precision.HIGHEST) / ROWS
    upper, r_inverse = factorize(gram)
    basis = jnp.einsum('kqc,qp->kpc', panel, r_inverse, precision=lax.Precision.HIGHEST)
    return (basis, upper)
```

```python
import functools

import jax
import jax.numpy as jnp
from jax import lax
from jax.experimental import pallas as pl
from jax.experimental.pallas import tpu as pltpu
from jax.sharding import PartitionSpec as P

BANDS = 4
HIGHEST = lax.Precision.HIGHEST
VMEM = pl.BlockSpec(memory_space=pltpu.VMEM)
LIMIT = 48 * 1024 * 1024


def struct(*shape):
    return jax.ShapeDtypeStruct(shape, jnp.float32)


def put(source, target, send, recv, probe, slab):
    return pltpu.make_async_remote_copy(
        src_ref=source,
        dst_ref=target,
        send_sem=send,
        recv_sem=recv,
        device_id=(probe, slab),
        device_id_type=pl.DeviceIdType.MESH,
    )


def greet(barrier, probe, slab):
    pl.semaphore_signal(
        barrier, inc=1, device_id=(probe, slab), device_id_type=pl.DeviceIdType.MESH
    )


def halo_kernel(probes, coefs, low, high, coef_low, coef_high, send, recv):
    mine, slab = lax.axis_index("probe"), lax.axis_index("slab")
    count = lax.axis_size("slab")
    after, before = lax.rem(slab + 1, count), lax.rem(slab + count - 1, count)
    barrier = pltpu.get_barrier_semaphore()
    greet(barrier, mine, after)
    greet(barrier, mine, before)
    pl.semaphore_wait(barrier, 2)
    cells = probes.shape[2]
    copies = [
        put(probes.at[:, :, cells - 128 :], low, send.at[0], recv.at[0], mine, after),
        put(probes.at[:, :, :128], high, send.at[1], recv.at[1], mine, before),
        put(coefs.at[:, cells - 128 :], coef_low, send.at[2], recv.at[2], mine, after),
        put(coefs.at[:, :128], coef_high, send.at[3], recv.at[3], mine, before),
    ]
    for copy in copies:
        copy.start()
    for copy in copies:
        copy.wait()


def exchange_halo(probes, coefs):
    edge = struct(probes.shape[0], probes.shape[1], 128)
    coef_edge = struct(coefs.shape[0], 128)
    return pl.pallas_call(
        halo_kernel,
        out_shape=(edge, edge, coef_edge, coef_edge),
        in_specs=[VMEM, VMEM],
        out_specs=(VMEM,) * 4,
        scratch_shapes=[pltpu.SemaphoreType.DMA((4,)), pltpu.SemaphoreType.DMA((4,))],
        compiler_params=pltpu.CompilerParams(collective_id=0, has_side_effects=True),
        name="halo",
    )(probes, coefs)


def stencil_kernel(offsets, field, low, high, coefs, coef_low, coef_high, out, spread):
    tiles = field.shape[2] // 128
    ring = tiles + 1
    slab = lax.axis_index("slab")
    last = lax.axis_size("slab") - 1
    lanes = lax.broadcasted_iota(jnp.int32, (8, 128), 1)
    from_high = lanes < 64
    inside = jnp.logical_or(
        jnp.logical_and(from_high, slab < last),
        jnp.logical_and(jnp.logical_not(from_high), slab > 0),
    )

    @pl.when(pl.program_id(0) == 0)
    def _():
        for row in range(40):
            for tile in range(tiles):
                spread[tile, row] = jnp.broadcast_to(
                    coefs[row : row + 1, 128 * tile : 128 * tile + 128], (8, 128)
                )
            edge = jnp.where(
                from_high,
                jnp.broadcast_to(coef_high[row : row + 1, :], (8, 128)),
                jnp.broadcast_to(coef_low[row : row + 1, :], (8, 128)),
            )
            spread[tiles, row] = jnp.where(inside, edge, 0.0)
        for tile in range(ring):
            visc = spread[tile, 36]
            for comp in range(3):
                spread[tile, 37 + comp] = visc * (spread[tile, 37 + comp] * visc)

    def shifted(values, offset):
        turn = lax.rem(128 - offset, 128)
        turned = [pltpu.roll(value, turn, 1) for value in values]
        reach = lanes + offset
        past, ahead = reach > 127, reach < 0
        return [
            jnp.where(
                past,
                turned[(tile + 1) % ring],
                jnp.where(ahead, turned[(tile + ring - 1) % ring], turned[tile]),
            )
            for tile in range(ring)
        ]

    values = []
    for comp in range(3):
        own = [field[comp, :, 128 * tile : 128 * tile + 128] for tile in range(tiles)]
        edge = jnp.where(from_high, high[comp], low[comp])
        values.append(own + [jnp.where(inside, edge, 0.0)])
    for turn in range(2):
        total = [list(value) for value in values]
        for band in range(BANDS):
            moved = [shifted(value, offsets[band]) for value in values]
            for comp in range(3):
                for source in range(3):
                    for tile in range(ring):
                        coef = spread[tile, 9 * band + 3 * comp + source]
                        total[comp][tile] = total[comp][tile] + coef * moved[source][tile]
        scaled = [
            [spread[tile, 37 + comp] * total[comp][tile] for tile in range(ring)]
            for comp in range(3)
        ]
        values = [list(value) for value in scaled]
        for band in range(BANDS):
            for source in range(3):
                parts = []
                for tile in range(ring):
                    part = spread[tile, 9 * band + source] * scaled[0][tile]
                    part = part + spread[tile, 9 * band + 3 + source] * scaled[1][tile]
                    part = part + spread[tile, 9 * band + 6 + source] * scaled[2][tile]
                    parts.append(part)
                moved = shifted(parts, -offsets[band])
                for tile in range(ring):
                    values[source][tile] = values[source][tile] + moved[tile]
        if turn == 0:
            for comp in range(3):
                values[comp][tiles] = jnp.where(inside, values[comp][tiles], 0.0)
    for comp in range(3):
        for tile in range(tiles):
            out[tile, comp] = values[comp][tile]


def both_hessians(offsets, probes, low, high, coefs, coef_low, coef_high):
    comps, columns, cells = probes.shape
    tiles = cells // 128
    rows = lambda i: (0, i, 0)
    whole = lambda i: (0, 0)
    return pl.pallas_call(
        stencil_kernel,
        grid=(columns // 8,),
        out_shape=struct(tiles, comps, columns, 128),
        in_specs=[
            pl.BlockSpec(memory_space=pltpu.SMEM),
            pl.BlockSpec((comps, 8, cells), rows),
            pl.BlockSpec((comps, 8, 128), rows),
            pl.BlockSpec((comps, 8, 128), rows),
            pl.BlockSpec(coefs.shape, whole),
            pl.BlockSpec(coef_low.shape, whole),
            pl.BlockSpec(coef_high.shape, whole),
        ],
        out_specs=pl.BlockSpec((tiles, comps, 8, 128), lambda i: (0, 0, i, 0)),
        scratch_shapes=[pltpu.VMEM((tiles + 1, coefs.shape[0], 8, 128), jnp.float32)],
        compiler_params=pltpu.CompilerParams(vmem_limit_bytes=LIMIT),
        name="stencil",
    )(offsets, probes, low, high, coefs, coef_low, coef_high)


def gram_kernel(
    panel, field, gram, part, half_in, half, eighth_in, eighth, tile_in, tile, gathered,
    swap_s, swap_r, core_s, core_r, fold_s, fold_r, spot_s, spot_r,
    line_s, line_r, back_s, back_r, pair_s, pair_r,
):
    mine, slab = lax.axis_index("probe"), lax.axis_index("slab")
    spot, core = slab // 2, lax.rem(slab, 2)
    twin = slab + 1 - 2 * core
    side, place = spot // 16, lax.rem(spot, 16)

    def group(step):
        return lax.rem(mine + step, 8)

    def source(step):
        return lax.rem(mine + 8 - step, 8)

    def far(step):
        return lax.rem(spot + step, 32)

    def line(step):
        return side * 16 + lax.rem(place + step, 16)

    barrier = pltpu.get_barrier_semaphore()
    greet(barrier, mine, twin)

    def greet_group(step, carry):
        greet(barrier, group(step), slab)
        return carry

    def greet_spot(step, carry):
        greet(barrier, mine, 2 * far(step) + core)
        return carry

    lax.fori_loop(1, 8, greet_group, 0)
    lax.fori_loop(1, 32, greet_spot, 0)
    pl.semaphore_wait(barrier, 39)

    def swap(step):
        return put(
            panel.at[group(step)], field.at[:, mine], swap_s.at[step], swap_r.at[step],
            group(step), slab,
        )

    def swap_start(step, carry):
        swap(step).start()
        return carry

    def swap_wait(step, carry):
        swap(step).wait()
        return carry

    lax.fori_loop(1, 8, swap_start, 0)
    field[:, mine] = panel[mine]
    lax.fori_loop(1, 8, swap_wait, 0)

    whole = jnp.concatenate([field[comp].reshape(512, 128) for comp in range(3)], 1)
    for lane in range(4):
        block = lax.dot_general(
            whole, whole[128 * lane : 128 * lane + 128], (((1,), (1,)), ((), ())),
            precision=HIGHEST, preferred_element_type=jnp.float32,
        )
        for row in range(8):
            part[lane // 2, row, 8 * (lane % 2) : 8 * (lane % 2) + 8] = block[
                64 * row : 64 * row + 64
            ].reshape(8, 8, 128)

    def to_twin(row):
        return put(
            part.at[1 - core, row], half_in.at[row], core_s.at[row], core_r.at[row], mine, twin
        )

    def twin_start(row, carry):
        to_twin(row).start()
        return carry

    lax.fori_loop(0, 8, twin_start, 0)

    def fold(step):
        return put(
            half.at[group(step)], eighth_in.at[mine], fold_s.at[step], fold_r.at[step],
            group(step), slab,
        )

    def twin_wait(row, carry):
        to_twin(row).wait()
        half[row] = part[core, row] + half_in[row]
        return carry

    lax.fori_loop(0, 8, twin_wait, 0)

    def fold_go(step, carry):
        fold(step).start()
        return carry

    def fold_wait(step, carry):
        fold(step).wait()
        return carry

    lax.fori_loop(1, 8, fold_go, 0)
    eighth_in[mine] = half[mine]
    lax.fori_loop(1, 8, fold_wait, 0)
    total = eighth_in[0]
    for row in range(1, 8):
        total = total + eighth_in[row]
    eighth[...] = total

    def scatter(step):
        return put(
            eighth.at[lax.rem(far(step), 16)], tile_in.at[spot], spot_s.at[step],
            spot_r.at[step], mine, 2 * far(step) + core,
        )

    def scatter_start(step, carry):
        scatter(step).start()
        return carry

    def scatter_wait(step, carry):
        scatter(step).wait()
        return carry

    lax.fori_loop(1, 32, scatter_start, 0)
    tile_in[spot] = eighth[place]
    lax.fori_loop(1, 32, scatter_wait, 0)
    total = tile_in[0]
    for row in range(1, 32):
        total = total + tile_in[row]
    tile[...] = total

    def spread_line(step):
        return put(
            tile, gathered.at[place], line_s.at[step], line_r.at[step], mine,
            2 * line(step) + core,
        )

    def line_start(step, carry):
        spread_line(step).start()
        return carry

    def line_wait(step, carry):
        spread_line(step).wait()
        return carry

    lax.fori_loop(1, 16, line_start, 0)
    gathered[place] = total
    lax.fori_loop(1, 16, line_wait, 0)

    def unfold(step):
        return put(
            gathered, gram.at[core, mine], back_s.at[step], back_r.at[step], group(step), slab
        )

    def unfold_start(step, carry):
        unfold(step).start()
        return carry

    lax.fori_loop(1, 8, unfold_start, 0)

    def pair(step):
        row = source(step)
        return put(
            gram.at[core, row], gram.at[core, row], pair_s.at[step], pair_r.at[step], mine, twin
        )

    gram[core, mine] = gathered[...]
    pair(0).start()

    def unfold_wait(step, carry):
        unfold(step).wait()
        pair(step).start()
        return carry

    lax.fori_loop(1, 8, unfold_wait, 0)

    def pair_wait(step, carry):
        pair(step).wait()
        return carry

    lax.fori_loop(0, 8, pair_wait, 0)


def summed_gram(panel):
    tiles, comps, columns, _ = panel.shape
    dma = lambda count: pltpu.SemaphoreType.DMA((count,))
    vmem = lambda *shape: pltpu.VMEM(shape, jnp.float32)
    return pl.pallas_call(
        gram_kernel,
        out_shape=(struct(comps, 8, columns, 128), struct(2, 8, 16, 8, 128)),
        in_specs=[VMEM],
        out_specs=(VMEM, VMEM),
        scratch_shapes=[
            vmem(2, 8, 16, 8, 128),
            vmem(8, 16, 8, 128),
            vmem(8, 16, 8, 128),
            vmem(8, 16, 8, 128),
            vmem(16, 8, 128),
            vmem(32, 8, 128),
            vmem(8, 128),
            vmem(16, 8, 128),
        ]
        + [dma(8)] * 6
        + [dma(32)] * 2
        + [dma(16)] * 2
        + [dma(8)] * 4,
        compiler_params=pltpu.CompilerParams(
            collective_id=1, has_side_effects=True, vmem_limit_bytes=LIMIT
        ),
        name="gram",
    )(panel)


def spread_row(value, row):
    return jnp.broadcast_to(value[row : row + 1, :], value.shape)


def eliminate(block, base):
    rows = lax.broadcasted_iota(jnp.int32, (8, 128), 0)
    work = [block[8 * i : 8 * i + 8] for i in range(8)]
    for turn in range(8):
        columns = {
            i: [
                jnp.broadcast_to(
                    work[i][:, base + 8 * turn + s : base + 8 * turn + s + 1], (8, 128)
                )
                for s in range(8)
            ]
            for i in range(turn, 8)
        }
        pivots = jnp.ones((8, 128), jnp.float32)
        for s in range(8):
            pivot = spread_row(columns[turn][s], s)
            inverse = 1.0 / pivot
            pivots = jnp.where(rows == s, pivot, pivots)
            lead = spread_row(work[turn], s)
            leads = {q: spread_row(columns[turn][q], s) for q in range(s + 1, 8)}
            for i in range(turn, 8):
                ratio = columns[i][s] * inverse
                if i == turn:
                    ratio = jnp.where(rows > s, ratio, 0.0)
                work[i] = work[i] - ratio * lead
                for q in range(s + 1, 8):
                    columns[i][q] = columns[i][q] - ratio * leads[q]
        work[turn] = work[turn] * lax.rsqrt(pivots)
    return jnp.concatenate(work, 0)


def factor_kernel(scale, gram, field, r_rows, basis, work, upper_all):
    size = 512
    for lane in range(4):
        for row in range(8):
            work[64 * row : 64 * row + 64, 128 * lane : 128 * lane + 128] = (
                gram[lane // 2, row, 8 * (lane % 2) : 8 * (lane % 2) + 8].reshape(64, 128) * scale
            )
    for comp in range(3):
        work[:, size + 128 * comp : size + 128 * comp + 128] = field[comp].reshape(size, 128)
    upper_all[...] = jnp.zeros_like(upper_all)
    lanes = lax.broadcasted_iota(jnp.int32, (64, 128), 1)
    rows = lax.broadcasted_iota(jnp.int32, (64, 128), 0)
    for step in range(8):
        lo, hi = 64 * step, 64 * step + 64
        base = 64 * (step % 2)
        tile = 128 * (step // 2)
        own = jnp.logical_and(lanes >= base, lanes < base + 64)
        unit = (lanes == rows + (64 - base)).astype(jnp.float32)
        done = eliminate(jnp.where(own, work[lo:hi, tile : tile + 128], unit), base)
        triangle = jnp.where(jnp.logical_and(own, lanes - base >= rows), done, 0.0)
        left = jnp.where(own, 0.0, done)
        start = 128 * (hi // 128)
        strip = work[lo:hi, start:]
        upper = jnp.dot(
            left, jnp.concatenate([strip, strip], 0), precision=HIGHEST,
            preferred_element_type=jnp.float32,
        )
        for comp in range(3):
            at = size - start + 128 * comp
            basis[step, comp] = upper[:, at : at + 128]
        if start < size:
            upper_all[lo:hi, start:] = upper[:, : size - start]
        upper_all[lo:hi, tile : tile + 128] = (
            triangle if base else jnp.where(own, triangle, upper[:, :128])
        )
        if hi < size:
            trail = lax.dot_general(
                upper[:, : size - start], upper, (((0,), (0,)), ((), ())), precision=HIGHEST,
                preferred_element_type=jnp.float32,
            )
            work[hi:, start:] = work[hi:, start:] - trail[hi - start :]
    mine = lax.axis_index("probe")
    r_rows[...] = upper_all[pl.ds(pl.multiple_of(64 * mine, 64), 64), :]


def factor(gram, field, unknowns):
    return pl.pallas_call(
        functools.partial(factor_kernel, 1.0 / unknowns),
        out_shape=(struct(64, 512), struct(8, 3, 64, 128)),
        in_specs=[VMEM, VMEM],
        out_specs=(VMEM, VMEM),
        scratch_shapes=[
            pltpu.VMEM((512, 896), jnp.float32),
            pltpu.VMEM((512, 512), jnp.float32),
        ],
        compiler_params=pltpu.CompilerParams(vmem_limit_bytes=LIMIT),
        name="factor",
    )(gram, field)


def return_kernel(blocks, basis, send, recv):
    mine, slab = lax.axis_index("probe"), lax.axis_index("slab")

    def group(step):
        return lax.rem(mine + step, 8)

    barrier = pltpu.get_barrier_semaphore()

    def greet_group(step, carry):
        greet(barrier, group(step), slab)
        return carry

    lax.fori_loop(1, 8, greet_group, 0)
    pl.semaphore_wait(barrier, 7)
    lanes = pl.ds(pl.multiple_of(128 * mine, 128), 128)

    def copy(step):
        return put(
            blocks.at[group(step)], basis.at[:, :, lanes], send.at[step], recv.at[step],
            group(step), slab,
        )

    def start(step, carry):
        copy(step).start()
        return carry

    def wait(step, carry):
        copy(step).wait()
        return carry

    lax.fori_loop(1, 8, start, 0)
    basis[:, :, lanes] = blocks[mine]
    lax.fori_loop(1, 8, wait, 0)


def return_blocks(blocks):
    tiles, comps, columns, width = blocks.shape
    return pl.pallas_call(
        return_kernel,
        out_shape=struct(comps, columns, tiles * width),
        in_specs=[VMEM],
        out_specs=VMEM,
        scratch_shapes=[pltpu.SemaphoreType.DMA((8,)), pltpu.SemaphoreType.DMA((8,))],
        compiler_params=pltpu.CompilerParams(collective_id=2, has_side_effects=True),
        name="return_blocks",
    )(blocks)


def body(probes, viscosity, coupling, misfit_weight, band_offsets):
    cells = probes.shape[2]
    unknowns = 3 * cells * lax.axis_size("slab")
    coefs = jnp.concatenate(
        [coupling.reshape(9 * BANDS, cells), viscosity[None, :], misfit_weight], 0
    )
    low, high, coef_low, coef_high = exchange_halo(probes, coefs)
    panel = both_hessians(band_offsets, probes, low, high, coefs, coef_low, coef_high)
    field, gram = summed_gram(panel)
    r_rows, blocks = factor(gram, field, unknowns)
    return (return_blocks(blocks), r_rows)


def solution(mesh):
    return jax.shard_map(
        body,
        mesh=mesh,
        in_specs=(
            P(None, "probe", "slab"),
            P("slab"),
            P(None, None, None, "slab"),
            P(None, "slab"),
            P(),
        ),
        out_specs=(P(None, "probe", "slab"), P("probe", None)),
        check_vma=False,
    )
```

```python
import functools

import jax
import jax.numpy as jnp
from jax import lax
from jax.experimental import pallas as pl
from jax.experimental.pallas import tpu as pltpu
from jax.sharding import PartitionSpec as P

BANDS = 4
HIGHEST = lax.Precision.HIGHEST
VMEM = pl.BlockSpec(memory_space=pltpu.VMEM)
HBM = pl.BlockSpec(memory_space=pltpu.HBM)
LIMIT = 48 * 1024 * 1024


def struct(*shape):
    return jax.ShapeDtypeStruct(shape, jnp.float32)


def put(source, target, send, recv, probe, slab):
    return pltpu.make_async_remote_copy(
        src_ref=source,
        dst_ref=target,
        send_sem=send,
        recv_sem=recv,
        device_id=(probe, slab),
        device_id_type=pl.DeviceIdType.MESH,
    )


def greet(barrier, probe, slab):
    pl.semaphore_signal(
        barrier, inc=1, device_id=(probe, slab), device_id_type=pl.DeviceIdType.MESH
    )


SIDE_CHUNKS = [(row, lane) for row in range(8) for lane in range(row // 2, 4)]


def tile_place(tile):
    return tile // 80, tile % 80 // 5, tile % 5


def front_kernel(
    offsets, probes_in, coupling_in, viscosity_in, weight_in, field, gram,
    probes, coupling, viscosity, weight, low, high, coup_low, coup_high, visc_low, visc_high, weight_low, weight_high,
    spread, panel, part, half_in, half, plane_in, piece, line_in, total,
    halo_s, halo_r, swap_s, swap_r, core_s, core_r, fold_s, fold_r,
    line_s, line_r, back_s, back_r, pair_s, pair_r, load,
):
    loads = [
        pltpu.make_async_copy(coupling_in, coupling, load.at[0]),
        pltpu.make_async_copy(viscosity_in, viscosity, load.at[1]),
        pltpu.make_async_copy(weight_in, weight, load.at[2]),
        pltpu.make_async_copy(probes_in, probes, load.at[3]),
    ]
    for copy in loads:
        copy.start()
    mine, slab = lax.axis_index("probe"), lax.axis_index("slab")
    count = lax.axis_size("slab")
    after, before = lax.rem(slab + 1, count), lax.rem(slab + count - 1, count)
    core, chip = lax.rem(slab, 2), slab // 2
    side, place = chip // 16, lax.rem(chip, 16)
    twin = slab + 1 - 2 * core
    rank = side * 8 + mine
    cells = probes.shape[2]
    tiles = cells // 128
    ring = tiles + 1

    def group(step):
        return lax.rem(mine + step, 8)

    def plane_rank(step):
        return lax.rem(rank + step, 16)

    def in_plane(step):
        other = plane_rank(step)
        return lax.rem(other, 8), 32 * (other // 8) + 2 * place + core

    def in_line(step):
        return mine, 32 * side + 2 * lax.rem(place + step, 16) + core

    barrier = pltpu.get_barrier_semaphore()
    greet(barrier, mine, after)
    greet(barrier, mine, before)

    def greet_rest(step, carry):
        greet(barrier, *in_plane(step))
        greet(barrier, *in_line(step))
        return carry

    lax.fori_loop(1, 16, greet_rest, 0)
    pl.semaphore_wait(barrier, 32)

    edge = pl.ds(cells - 128, 128)
    start = pl.ds(0, 128)
    copies = [
        put(probes_in.at[:, :, edge], low, halo_s.at[0], halo_r.at[0], mine, after),
        put(probes_in.at[:, :, start], high, halo_s.at[1], halo_r.at[1], mine, before),
        put(coupling_in.at[:, :, :, edge], coup_low, halo_s.at[2], halo_r.at[2], mine, after),
        put(coupling_in.at[:, :, :, start], coup_high, halo_s.at[3], halo_r.at[3], mine, before),
        put(viscosity_in.at[:, edge], visc_low, halo_s.at[4], halo_r.at[4], mine, after),
        put(viscosity_in.at[:, start], visc_high, halo_s.at[5], halo_r.at[5], mine, before),
        put(weight_in.at[:, edge], weight_low, halo_s.at[6], halo_r.at[6], mine, after),
        put(weight_in.at[:, start], weight_high, halo_s.at[7], halo_r.at[7], mine, before),
    ]
    for copy in copies:
        copy.start()

    lanes = lax.broadcasted_iota(jnp.int32, (8, 128), 1)
    from_high = lanes < 64
    inside = jnp.logical_or(
        jnp.logical_and(from_high, slab < count - 1),
        jnp.logical_and(jnp.logical_not(from_high), slab > 0),
    )

    def wide(value):
        return jnp.broadcast_to(value, (8, 128))

    def fill(tile, coup, visc, wt):
        for band in range(BANDS):
            for comp in range(3):
                for source in range(3):
                    spread[tile, 9 * band + 3 * comp + source] = coup(comp, source, band)
        for comp in range(3):
            spread[tile, 36 + comp] = visc * (wt(comp) * visc)

    for copy in loads:
        copy.wait()
    for tile in range(tiles):
        at = slice(128 * tile, 128 * tile + 128)
        fill(
            tile,
            lambda comp, source, band: wide(coupling[comp, source, band : band + 1, at]),
            wide(viscosity[:, at]),
            lambda comp: wide(weight[comp : comp + 1, at]),
        )
    for copy in copies:
        copy.wait()

    def merged(below, above):
        return jnp.where(inside, jnp.where(from_high, wide(above), wide(below)), 0.0)

    fill(
        tiles,
        lambda comp, source, band: merged(
            coup_low[comp, source, band : band + 1], coup_high[comp, source, band : band + 1]
        ),
        merged(visc_low[...], visc_high[...]),
        lambda comp: merged(weight_low[comp : comp + 1], weight_high[comp : comp + 1]),
    )

    def shifted(values, offset):
        turned = [pltpu.roll(value, lax.rem(128 - offset, 128), 1) for value in values]
        reach = lanes + offset
        past, ahead = reach > 127, reach < 0
        return [
            jnp.where(
                past,
                turned[(tile + 1) % ring],
                jnp.where(ahead, turned[(tile + ring - 1) % ring], turned[tile]),
            )
            for tile in range(ring)
        ]

    def swap(step, rows, at):
        return put(
            panel.at[group(step), :, rows, :], field.at[:, mine, rows, :],
            swap_s.at[step], swap_r.at[step], group(step), slab,
        )

    def probe_rows(at, carry):
        rows = pl.ds(pl.multiple_of(8 * at, 8), 8)
        values = []
        for comp in range(3):
            own = [probes[comp, rows, 128 * tile : 128 * tile + 128] for tile in range(tiles)]
            ends = jnp.where(from_high, high[comp, rows, :], low[comp, rows, :])
            values.append(own + [jnp.where(inside, ends, 0.0)])
        for turn in range(2):
            result = [list(value) for value in values]
            for band in range(BANDS):
                moved = [shifted(value, offsets[band]) for value in values]
                for comp in range(3):
                    for source in range(3):
                        for tile in range(ring):
                            coef = spread[tile, 9 * band + 3 * comp + source]
                            result[comp][tile] = result[comp][tile] + coef * moved[source][tile]
            scaled = [
                [spread[tile, 36 + comp] * result[comp][tile] for tile in range(ring)]
                for comp in range(3)
            ]
            values = [list(value) for value in scaled]
            for band in range(BANDS):
                for source in range(3):
                    parts = []
                    for tile in range(ring):
                        term = spread[tile, 9 * band + source] * scaled[0][tile]
                        term = term + spread[tile, 9 * band + 3 + source] * scaled[1][tile]
                        term = term + spread[tile, 9 * band + 6 + source] * scaled[2][tile]
                        parts.append(term)
                    moved = shifted(parts, -offsets[band])
                    for tile in range(ring):
                        values[source][tile] = values[source][tile] + moved[tile]
            if turn == 0:
                for comp in range(3):
                    values[comp][tiles] = jnp.where(inside, values[comp][tiles], 0.0)
        for comp in range(3):
            for tile in range(tiles):
                panel[tile, comp, rows, :] = values[comp][tile]

        def send(step, inner):
            swap(step, rows, at).start()
            return inner

        lax.fori_loop(1, 8, send, 0)
        return carry

    lax.fori_loop(0, probes.shape[1] // 8, probe_rows, 0)
    field[:, mine] = panel[mine]
    every = pl.ds(0, probes.shape[1])

    def swap_wait(step, carry):
        swap(step, every, 0).wait()
        return carry

    lax.fori_loop(1, 8, swap_wait, 0)

    whole = jnp.concatenate([field[comp].reshape(512, 128) for comp in range(3)], 1)
    blocks = [
        lax.dot_general(
            whole[: 128 * lane + 128], whole[128 * lane : 128 * lane + 128],
            (((1,), (1,)), ((), ())), precision=HIGHEST, preferred_element_type=jnp.float32,
        )
        for lane in range(4)
    ]
    for chunk, (row, lane) in enumerate(SIDE_CHUNKS):
        for i in range(8):
            at = 64 * row + 8 * i
            part[tile_place(8 * chunk + i)] = blocks[lane][at : at + 8]

    def to_twin(step):
        other = plane_rank(step)
        return put(
            part.at[1 - core, other], half_in.at[other], core_s.at[step], core_r.at[step],
            mine, twin,
        )

    def fold(step):
        return put(
            half.at[plane_rank(step)], plane_in.at[rank], fold_s.at[step], fold_r.at[step],
            *in_plane(step),
        )

    def twin_start(step, carry):
        to_twin(lax.rem(step, 16)).start()
        return carry

    def add_twin(step):
        other = plane_rank(step)
        to_twin(step).wait()
        half[other] = part[core, other] + half_in[other]

    def twin_wait(step, carry):
        add_twin(step)
        fold(step).start()
        return carry

    lax.fori_loop(1, 17, twin_start, 0)
    lax.fori_loop(1, 16, twin_wait, 0)
    add_twin(0)
    plane_in[rank] = half[rank]

    def fold_wait(step, carry):
        fold(step).wait()
        return carry

    lax.fori_loop(1, 16, fold_wait, 0)
    summed = plane_in[0]
    for other in range(1, 16):
        summed = summed + plane_in[other]
    piece[...] = summed

    def line(step):
        return put(
            piece, line_in.at[place], line_s.at[step], line_r.at[step], *in_line(step)
        )

    def line_start(step, carry):
        line(step).start()
        return carry

    def line_wait(step, carry):
        line(step).wait()
        return carry

    lax.fori_loop(1, 16, line_start, 0)
    line_in[place] = summed
    lax.fori_loop(1, 16, line_wait, 0)
    summed = line_in[0]
    for other in range(1, 16):
        summed = summed + line_in[other]
    total[...] = summed

    def back(step):
        return put(
            total, gram.at[core, rank], back_s.at[step], back_r.at[step], *in_plane(step)
        )

    def pair(step):
        other = lax.rem(rank + 16 - step, 16)
        return put(
            gram.at[core, other], gram.at[core, other], pair_s.at[step], pair_r.at[step],
            mine, twin,
        )

    def back_start(step, carry):
        back(step).start()
        return carry

    lax.fori_loop(1, 16, back_start, 0)
    gram[core, rank] = summed
    pair(0).start()

    def back_wait(step, carry):
        back(step).wait()
        pair(step).start()
        return carry

    lax.fori_loop(1, 16, back_wait, 0)

    def pair_wait(step, carry):
        pair(step).wait()
        return carry

    lax.fori_loop(0, 16, pair_wait, 0)


def front(offsets, probes, coupling, viscosity, weight):
    comps, columns, cells = probes.shape
    tiles = cells // 128
    dma = lambda count: pltpu.SemaphoreType.DMA((count,))
    vmem = lambda *shape: pltpu.VMEM(shape, jnp.float32)
    return pl.pallas_call(
        front_kernel,
        out_shape=(struct(comps, 8, columns, 128), struct(2, 16, 5, 8, 128)),
        in_specs=[pl.BlockSpec(memory_space=pltpu.SMEM)] + [HBM] * 4,
        out_specs=(VMEM, VMEM),
        scratch_shapes=[
            vmem(comps, columns, cells),
            vmem(3, 3, BANDS, cells),
            vmem(1, cells),
            vmem(3, cells),
            vmem(comps, columns, 128),
            vmem(comps, columns, 128),
            vmem(3, 3, BANDS, 128),
            vmem(3, 3, BANDS, 128),
            vmem(1, 128),
            vmem(1, 128),
            vmem(3, 128),
            vmem(3, 128),
            vmem(tiles + 1, 9 * BANDS + 3, 8, 128),
            vmem(tiles, comps, columns, 128),
            vmem(2, 16, 5, 8, 128),
            vmem(16, 5, 8, 128),
            vmem(16, 5, 8, 128),
            vmem(16, 5, 8, 128),
            vmem(5, 8, 128),
            vmem(16, 5, 8, 128),
            vmem(5, 8, 128),
        ]
        + [dma(8)] * 4
        + [dma(16)] * 10
        + [dma(4)],
        compiler_params=pltpu.CompilerParams(
            collective_id=0, has_side_effects=True, vmem_limit_bytes=61 * 1024 * 1024
        ),
        name="front",
    )(offsets, probes, coupling, viscosity, weight)


def spread_row(value, row):
    return jnp.broadcast_to(value[row : row + 1, :], value.shape)


def eliminate(block, base):
    rows = lax.broadcasted_iota(jnp.int32, (8, 128), 0)
    work = [block[8 * i : 8 * i + 8] for i in range(8)]
    for turn in range(8):
        columns = {
            i: [
                jnp.broadcast_to(
                    work[i][:, base + 8 * turn + s : base + 8 * turn + s + 1], (8, 128)
                )
                for s in range(8)
            ]
            for i in range(turn, 8)
        }
        pivots = jnp.ones((8, 128), jnp.float32)
        for s in range(8):
            pivot = spread_row(columns[turn][s], s)
            inverse = 1.0 / pivot
            pivots = jnp.where(rows == s, pivot, pivots)
            lead = spread_row(work[turn], s)
            leads = {q: spread_row(columns[turn][q], s) for q in range(s + 1, 8)}
            for i in range(turn, 8):
                ratio = columns[i][s] * inverse
                if i == turn:
                    ratio = jnp.where(rows > s, ratio, 0.0)
                work[i] = work[i] - ratio * lead
                for q in range(s + 1, 8):
                    columns[i][q] = columns[i][q] - ratio * leads[q]
        work[turn] = work[turn] * lax.rsqrt(pivots)
    return jnp.concatenate(work, 0)


def back_kernel(scale, gram, field, basis, r_rows, work, upper_all, blocks, send, recv):
    mine, slab = lax.axis_index("probe"), lax.axis_index("slab")

    def group(step):
        return lax.rem(mine + step, 8)

    barrier = pltpu.get_barrier_semaphore()

    def greet_group(step, carry):
        greet(barrier, group(step), slab)
        return carry

    lax.fori_loop(1, 8, greet_group, 0)
    size = 512
    for chunk, (row, lane) in enumerate(SIDE_CHUNKS):
        for i in range(8):
            at = 64 * row + 8 * i
            work[at : at + 8, 128 * lane : 128 * lane + 128] = (
                gram[tile_place(8 * chunk + i)] * scale
            )
    for comp in range(3):
        work[:, size + 128 * comp : size + 128 * comp + 128] = field[comp].reshape(size, 128)
    upper_all[...] = jnp.zeros_like(upper_all)
    lanes = lax.broadcasted_iota(jnp.int32, (64, 128), 1)
    rows = lax.broadcasted_iota(jnp.int32, (64, 128), 0)
    for step in range(8):
        lo, hi = 64 * step, 64 * step + 64
        base = 64 * (step % 2)
        tile = 128 * (step // 2)
        own = jnp.logical_and(lanes >= base, lanes < base + 64)
        unit = (lanes == rows + (64 - base)).astype(jnp.float32)
        done = eliminate(jnp.where(own, work[lo:hi, tile : tile + 128], unit), base)
        triangle = jnp.where(jnp.logical_and(own, lanes - base >= rows), done, 0.0)
        left = jnp.where(own, 0.0, done)
        start = 128 * (hi // 128)
        strip = work[lo:hi, start:]
        upper = jnp.dot(
            left, jnp.concatenate([strip, strip], 0), precision=HIGHEST,
            preferred_element_type=jnp.float32,
        )
        for comp in range(3):
            at = size - start + 128 * comp
            blocks[step, comp] = upper[:, at : at + 128]
        if start < size:
            upper_all[lo:hi, start:] = upper[:, : size - start]
        upper_all[lo:hi, tile : tile + 128] = (
            triangle if base else jnp.where(own, triangle, upper[:, :128])
        )
        if hi < size:
            trail = lax.dot_general(
                upper[:, : size - start], upper, (((0,), (0,)), ((), ())), precision=HIGHEST,
                preferred_element_type=jnp.float32,
            )
            work[hi:, start:] = work[hi:, start:] - trail[hi - start :]

    pl.semaphore_wait(barrier, 7)
    place = pl.ds(pl.multiple_of(128 * mine, 128), 128)

    def copy(step):
        return put(
            blocks.at[group(step)], basis.at[:, :, place], send.at[step], recv.at[step],
            group(step), slab,
        )

    def start_copy(step, carry):
        copy(step).start()
        return carry

    def wait_copy(step, carry):
        copy(step).wait()
        return carry

    lax.fori_loop(1, 8, start_copy, 0)
    basis[:, :, place] = blocks[mine]
    r_rows[...] = upper_all[pl.ds(pl.multiple_of(64 * mine, 64), 64), :]
    lax.fori_loop(1, 8, wait_copy, 0)


def factor_and_return(gram, field, unknowns):
    return pl.pallas_call(
        functools.partial(back_kernel, 1.0 / unknowns),
        out_shape=(struct(3, 64, 1024), struct(64, 512)),
        in_specs=[VMEM, VMEM],
        out_specs=(VMEM, VMEM),
        scratch_shapes=[
            pltpu.VMEM((512, 896), jnp.float32),
            pltpu.VMEM((512, 512), jnp.float32),
            pltpu.VMEM((8, 3, 64, 128), jnp.float32),
            pltpu.SemaphoreType.DMA((8,)),
            pltpu.SemaphoreType.DMA((8,)),
        ],
        compiler_params=pltpu.CompilerParams(
            collective_id=1, has_side_effects=True, vmem_limit_bytes=LIMIT
        ),
        name="factor_and_return",
    )(gram, field)


def place_kernel(basis, r_rows, basis_out, r_out):
    basis_out[...] = basis[...]
    r_out[...] = r_rows[...]


def placed(basis, r_rows):
    return pl.pallas_call(
        place_kernel,
        out_shape=(struct(*basis.shape), struct(*r_rows.shape)),
        in_specs=[VMEM, VMEM],
        out_specs=(VMEM, VMEM),
        compiler_params=pltpu.CompilerParams(vmem_limit_bytes=4 * 1024 * 1024),
        name="placed",
    )(basis, r_rows)


def body(probes, viscosity, coupling, misfit_weight, band_offsets):
    unknowns = 3 * probes.shape[2] * lax.axis_size("slab")
    field, gram = front(
        band_offsets, probes, coupling.transpose(1, 2, 0, 3), viscosity[None, :], misfit_weight
    )
    return placed(*factor_and_return(gram, field, unknowns))


def solution(mesh):
    return jax.shard_map(
        body,
        mesh=mesh,
        in_specs=(
            P(None, "probe", "slab"),
            P("slab"),
            P(None, None, None, "slab"),
            P(None, "slab"),
            P(),
        ),
        out_specs=(P(None, "probe", "slab"), P("probe", None)),
        check_vma=False,
    )
```

```python
import functools

import jax
import jax.numpy as jnp
from jax import lax
from jax.experimental import pallas as pl
from jax.experimental.pallas import tpu as pltpu
from jax.sharding import PartitionSpec as P

BANDS = 4
HIGHEST = lax.Precision.HIGHEST
VMEM = pl.BlockSpec(memory_space=pltpu.VMEM)
HBM = pl.BlockSpec(memory_space=pltpu.HBM)
LIMIT = 48 * 1024 * 1024


def struct(*shape):
    return jax.ShapeDtypeStruct(shape, jnp.float32)


def put(source, target, send, recv, probe, slab):
    return pltpu.make_async_remote_copy(
        src_ref=source,
        dst_ref=target,
        send_sem=send,
        recv_sem=recv,
        device_id=(probe, slab),
        device_id_type=pl.DeviceIdType.MESH,
    )


def greet(barrier, probe, slab):
    pl.semaphore_signal(
        barrier, inc=1, device_id=(probe, slab), device_id_type=pl.DeviceIdType.MESH
    )


SIDE_CHUNKS = [(row, lane) for row in range(8) for lane in range(row // 2, 4)]


def tile_place(tile):
    return tile // 80, tile % 80 // 5, tile % 5


def spread_row(value, row):
    return jnp.broadcast_to(value[row : row + 1, :], value.shape)


def eliminate(block, base, meanwhile):
    rows = lax.broadcasted_iota(jnp.int32, (8, 128), 0)
    work = [block[8 * i : 8 * i + 8] for i in range(8)]
    for turn in range(8):
        columns = {
            i: [
                jnp.broadcast_to(
                    work[i][:, base + 8 * turn + s : base + 8 * turn + s + 1], (8, 128)
                )
                for s in range(8)
            ]
            for i in range(turn, 8)
        }
        pivots = jnp.ones((8, 128), jnp.float32)
        for s in range(8):
            pivot = spread_row(columns[turn][s], s)
            inverse = 1.0 / pivot
            pivots = jnp.where(rows == s, pivot, pivots)
            lead = spread_row(work[turn], s)
            leads = {q: spread_row(columns[turn][q], s) for q in range(s + 1, 8)}
            for i in range(turn, 8):
                ratio = columns[i][s] * inverse
                if i == turn:
                    ratio = jnp.where(rows > s, ratio, 0.0)
                work[i] = work[i] - ratio * lead
                for q in range(s + 1, 8):
                    columns[i][q] = columns[i][q] - ratio * leads[q]
        work[turn] = work[turn] * lax.rsqrt(pivots)
        count = len(meanwhile)
        for item in meanwhile[count * turn // 8 : count * (turn + 1) // 8]:
            item()
    return jnp.concatenate(work, 0)


def product(left, right, dims):
    return lax.dot_general(
        left, right, (dims, ((), ())), precision=HIGHEST, preferred_element_type=jnp.float32
    )


def factorize(work, upper_all, blocks):
    size, width = 512, 896
    lanes = lax.broadcasted_iota(jnp.int32, (64, 128), 1)
    rows = lax.broadcasted_iota(jnp.int32, (64, 128), 0)
    block = work[0:64, 0:128]
    meanwhile = []
    for step in range(8):
        lo, hi = 64 * step, 64 * step + 64
        base = 64 * (step % 2)
        tile = 128 * (step // 2)
        own = jnp.logical_and(lanes >= base, lanes < base + 64)
        unit = (lanes == rows + (64 - base)).astype(jnp.float32)
        done = eliminate(jnp.where(own, block, unit), base, meanwhile)
        triangle = jnp.where(jnp.logical_and(own, lanes - base >= rows), done, 0.0)
        left = jnp.where(own, 0.0, done)
        start = 128 * (hi // 128)

        def upper_of(at, count, lo=lo, hi=hi, left=left):
            strip = work[lo:hi, at : at + count]
            return product(left, jnp.concatenate([strip, strip], 0), ((1,), (0,)))

        if hi == size:
            upper_all[lo:hi, tile : tile + 128] = triangle
            last = upper_of(size, 384)
            for comp in range(3):
                blocks[step, comp] = last[:, 128 * comp : 128 * comp + 128]
            break
        first = upper_of(start, 128)
        trail = product(first, first, ((0,), (0,)))
        block = work[hi : hi + 64, start : start + 128] - trail[hi - start : hi - start + 64]
        upper = {start: first}
        meanwhile = []
        spans = [(at, min(256, size - at)) for at in range(start + 128, size, 256)]
        spans += [(size, 256), (size + 256, 128)]

        def keep(lo=lo, hi=hi, base=base, tile=tile, own=own, triangle=triangle, first=first, start=start):
            if base == 0:
                upper_all[lo:hi, tile : tile + 128] = jnp.where(own, triangle, first)
            else:
                upper_all[lo:hi, tile : tile + 128] = triangle
                upper_all[lo:hi, start : start + 128] = first

        def solve(at, count, step=step, lo=lo, hi=hi, upper=upper, upper_of=upper_of):
            value = upper_of(at, count)
            for part in range(at, at + count, 128):
                piece = value[:, part - at : part - at + 128]
                upper[part] = piece
                if part < size:
                    upper_all[lo:hi, part : part + 128] = piece
                else:
                    blocks[step, (part - size) // 128] = piece

        def update(at, count, hi=hi, start=start, upper=upper):
            reach = min(size, at + count)
            left_side = jnp.concatenate([upper[part] for part in range(start, reach, 128)], 1)
            right_side = jnp.concatenate([upper[part] for part in range(at, at + count, 128)], 1)
            trail = product(left_side, right_side, ((0,), (0,)))
            work[hi:reach, at : at + count] = work[hi:reach, at : at + count] - trail[hi - start :]

        meanwhile.append(keep)
        solves = [functools.partial(solve, at, count) for at, count in spans]
        updates = [functools.partial(update, at, count) for at, count in spans]
        if base:
            def below(hi=hi, start=start, trail=trail):
                work[hi + 64 : start + 128, start : start + 128] = (
                    work[hi + 64 : start + 128, start : start + 128] - trail[hi + 64 - start :]
                )
            meanwhile.append(below)
        if base:
            def beside(hi=hi, start=start, block=block):
                work[hi : hi + 64, start : start + 128] = block
            meanwhile.append(beside)
        meanwhile += solves + updates


def whole_kernel(
    scale,
    offsets, probes_in, coupling_in, viscosity_in, weight_in, basis, r_rows,
    field, gram, work, upper_all, blocks, probes, coupling, viscosity, weight, low, high, coup_low, coup_high, visc_low, visc_high, weight_low, weight_high,
    spread, panel, part, half_in, half, plane_in, piece, near_in, near, line_in, total,
    halo_s, halo_r, swap_s, swap_r, core_s, core_r, fold_s, fold_r,
    near_s, near_r, line_s, line_r, back_s, back_r, pair_s, pair_r, load, send, recv,
):
    loads = [
        pltpu.make_async_copy(coupling_in, coupling, load.at[0]),
        pltpu.make_async_copy(viscosity_in, viscosity, load.at[1]),
        pltpu.make_async_copy(weight_in, weight, load.at[2]),
        pltpu.make_async_copy(probes_in, probes, load.at[3]),
    ]
    for copy in loads:
        copy.start()
    mine, slab = lax.axis_index("probe"), lax.axis_index("slab")
    count = lax.axis_size("slab")
    after, before = lax.rem(slab + 1, count), lax.rem(slab + count - 1, count)
    core, chip = lax.rem(slab, 2), slab // 2
    side, place = chip // 16, lax.rem(chip, 16)
    twin = slab + 1 - 2 * core
    rank = side * 8 + mine
    cells = probes.shape[2]
    tiles = cells // 128
    ring = tiles + 1

    def group(step):
        return lax.rem(mine + step, 8)

    def plane_rank(step):
        return lax.rem(rank + step, 16)

    def in_plane(step):
        other = plane_rank(step)
        return lax.rem(other, 8), 32 * (other // 8) + 2 * place + core

    quad, spot = place // 4, lax.rem(place, 4)

    def in_quad(step):
        return mine, 32 * side + 2 * (4 * quad + lax.rem(spot + step, 4)) + core

    def in_line(step):
        return mine, 32 * side + 2 * (4 * lax.rem(quad + step, 4) + spot) + core

    barrier = pltpu.get_barrier_semaphore()
    greet(barrier, mine, after)
    greet(barrier, mine, before)

    def greet_plane(step, carry):
        greet(barrier, *in_plane(step))
        return carry

    def greet_line(step, carry):
        greet(barrier, *in_quad(step))
        greet(barrier, *in_line(step))
        return carry

    lax.fori_loop(1, 4, greet_line, 0)
    lax.fori_loop(1, 16, greet_plane, 0)
    pl.semaphore_wait(barrier, 23)

    edge = pl.ds(cells - 128, 128)
    start = pl.ds(0, 128)
    copies = [
        put(probes_in.at[:, :, edge], low, halo_s.at[0], halo_r.at[0], mine, after),
        put(probes_in.at[:, :, start], high, halo_s.at[1], halo_r.at[1], mine, before),
        put(coupling_in.at[:, :, :, edge], coup_low, halo_s.at[2], halo_r.at[2], mine, after),
        put(coupling_in.at[:, :, :, start], coup_high, halo_s.at[3], halo_r.at[3], mine, before),
        put(viscosity_in.at[:, edge], visc_low, halo_s.at[4], halo_r.at[4], mine, after),
        put(viscosity_in.at[:, start], visc_high, halo_s.at[5], halo_r.at[5], mine, before),
        put(weight_in.at[:, edge], weight_low, halo_s.at[6], halo_r.at[6], mine, after),
        put(weight_in.at[:, start], weight_high, halo_s.at[7], halo_r.at[7], mine, before),
    ]
    for copy in copies:
        copy.start()

    lanes = lax.broadcasted_iota(jnp.int32, (8, 128), 1)
    from_high = lanes < 64
    inside = jnp.logical_or(
        jnp.logical_and(from_high, slab < count - 1),
        jnp.logical_and(jnp.logical_not(from_high), slab > 0),
    )

    def wide(value):
        return jnp.broadcast_to(value, (8, 128))

    def fill(tile, coup, visc, wt):
        for band in range(BANDS):
            for comp in range(3):
                for source in range(3):
                    spread[tile, 9 * band + 3 * comp + source] = coup(comp, source, band)
        for comp in range(3):
            spread[tile, 36 + comp] = visc * (wt(comp) * visc)

    for copy in loads:
        copy.wait()
    for tile in range(tiles):
        at = slice(128 * tile, 128 * tile + 128)
        fill(
            tile,
            lambda comp, source, band: wide(coupling[comp, source, band : band + 1, at]),
            wide(viscosity[:, at]),
            lambda comp: wide(weight[comp : comp + 1, at]),
        )
    for copy in copies:
        copy.wait()

    def merged(below, above):
        return jnp.where(inside, jnp.where(from_high, wide(above), wide(below)), 0.0)

    fill(
        tiles,
        lambda comp, source, band: merged(
            coup_low[comp, source, band : band + 1], coup_high[comp, source, band : band + 1]
        ),
        merged(visc_low[...], visc_high[...]),
        lambda comp: merged(weight_low[comp : comp + 1], weight_high[comp : comp + 1]),
    )

    def shifted(values, offset):
        turned = [pltpu.roll(value, lax.rem(128 - offset, 128), 1) for value in values]
        reach = lanes + offset
        past, ahead = reach > 127, reach < 0
        return [
            jnp.where(
                past,
                turned[(tile + 1) % ring],
                jnp.where(ahead, turned[(tile + ring - 1) % ring], turned[tile]),
            )
            for tile in range(ring)
        ]

    def swap(step, rows, at):
        return put(
            panel.at[group(step), :, rows, :], field.at[:, mine, rows, :],
            swap_s.at[step], swap_r.at[step], group(step), slab,
        )

    def probe_rows(at, carry):
        rows = pl.ds(pl.multiple_of(8 * at, 8), 8)
        values = []
        for comp in range(3):
            own = [probes[comp, rows, 128 * tile : 128 * tile + 128] for tile in range(tiles)]
            ends = jnp.where(from_high, high[comp, rows, :], low[comp, rows, :])
            values.append(own + [jnp.where(inside, ends, 0.0)])
        for turn in range(2):
            result = [list(value) for value in values]
            for band in range(BANDS):
                moved = [shifted(value, offsets[band]) for value in values]
                for comp in range(3):
                    for source in range(3):
                        for tile in range(ring):
                            coef = spread[tile, 9 * band + 3 * comp + source]
                            result[comp][tile] = result[comp][tile] + coef * moved[source][tile]
            scaled = [
                [spread[tile, 36 + comp] * result[comp][tile] for tile in range(ring)]
                for comp in range(3)
            ]
            values = [list(value) for value in scaled]
            for band in range(BANDS):
                for source in range(3):
                    parts = []
                    for tile in range(ring):
                        term = spread[tile, 9 * band + source] * scaled[0][tile]
                        term = term + spread[tile, 9 * band + 3 + source] * scaled[1][tile]
                        term = term + spread[tile, 9 * band + 6 + source] * scaled[2][tile]
                        parts.append(term)
                    moved = shifted(parts, -offsets[band])
                    for tile in range(ring):
                        values[source][tile] = values[source][tile] + moved[tile]
            if turn == 0:
                for comp in range(3):
                    values[comp][tiles] = jnp.where(inside, values[comp][tiles], 0.0)
        for comp in range(3):
            for tile in range(tiles):
                panel[tile, comp, rows, :] = values[comp][tile]

        def send(step, inner):
            swap(step, rows, at).start()
            return inner

        lax.fori_loop(1, 8, send, 0)
        return carry

    lax.fori_loop(0, probes.shape[1] // 8, probe_rows, 0)
    field[:, mine] = panel[mine]
    every = pl.ds(0, probes.shape[1])

    def swap_wait(step, carry):
        swap(step, every, 0).wait()
        return carry

    lax.fori_loop(1, 8, swap_wait, 0)

    whole = jnp.concatenate([field[comp].reshape(512, 128) for comp in range(3)], 1)
    products = [
        lax.dot_general(
            whole[: 128 * lane + 128], whole[128 * lane : 128 * lane + 128],
            (((1,), (1,)), ((), ())), precision=HIGHEST, preferred_element_type=jnp.float32,
        )
        for lane in range(4)
    ]
    for chunk, (row, lane) in enumerate(SIDE_CHUNKS):
        for i in range(8):
            at = 64 * row + 8 * i
            part[tile_place(8 * chunk + i)] = products[lane][at : at + 8]

    def to_twin(step):
        other = plane_rank(step)
        return put(
            part.at[1 - core, other], half_in.at[other], core_s.at[step], core_r.at[step],
            mine, twin,
        )

    def fold(step):
        return put(
            half.at[plane_rank(step)], plane_in.at[rank], fold_s.at[step], fold_r.at[step],
            *in_plane(step),
        )

    def twin_start(step, carry):
        to_twin(lax.rem(step, 16)).start()
        return carry

    def add_twin(step):
        other = plane_rank(step)
        to_twin(step).wait()
        half[other] = part[core, other] + half_in[other]

    def twin_wait(step, carry):
        add_twin(step)
        fold(step).start()
        return carry

    lax.fori_loop(1, 17, twin_start, 0)
    lax.fori_loop(1, 16, twin_wait, 0)
    add_twin(0)
    plane_in[rank] = half[rank]

    def fold_wait(step, carry):
        fold(step).wait()
        return carry

    lax.fori_loop(1, 16, fold_wait, 0)
    summed = plane_in[0]
    for other in range(1, 16):
        summed = summed + plane_in[other]
    piece[...] = summed

    def close_by(step):
        return put(
            piece, near_in.at[spot], near_s.at[step], near_r.at[step], *in_quad(step)
        )

    def line(step):
        return put(
            near, line_in.at[quad], line_s.at[step], line_r.at[step], *in_line(step)
        )

    for step in range(1, 4):
        close_by(step).start()
    near_in[spot] = summed
    for step in range(1, 4):
        close_by(step).wait()
    summed = near_in[0] + near_in[1] + near_in[2] + near_in[3]
    near[...] = summed
    for step in range(1, 4):
        line(step).start()
    line_in[quad] = summed
    for step in range(1, 4):
        line(step).wait()
    summed = line_in[0] + line_in[1] + line_in[2] + line_in[3]
    total[...] = summed

    def back(step):
        return put(
            total, gram.at[core, rank], back_s.at[step], back_r.at[step], *in_plane(step)
        )

    def pair(step):
        other = lax.rem(rank + 16 - step, 16)
        return put(
            gram.at[core, other], gram.at[core, other], pair_s.at[step], pair_r.at[step],
            mine, twin,
        )

    def back_start(step, carry):
        back(step).start()
        return carry

    lax.fori_loop(1, 16, back_start, 0)
    size = 512
    for comp in range(3):
        work[:, size + 128 * comp : size + 128 * comp + 128] = field[comp].reshape(size, 128)
    upper_all[...] = jnp.zeros_like(upper_all)
    gram[core, rank] = summed
    pair(0).start()

    def back_wait(step, carry):
        back(step).wait()
        pair(step).start()
        return carry

    lax.fori_loop(1, 16, back_wait, 0)

    def pair_wait(step, carry):
        pair(step).wait()
        return carry

    lax.fori_loop(0, 16, pair_wait, 0)

    for chunk, (row, lane) in enumerate(SIDE_CHUNKS):
        for i in range(8):
            at = 64 * row + 8 * i
            work[at : at + 8, 128 * lane : 128 * lane + 128] = (
                gram[tile_place(8 * chunk + i)] * scale
            )
    factorize(work, upper_all, blocks)

    home = pl.ds(pl.multiple_of(128 * mine, 128), 128)

    def give(step):
        return put(
            blocks.at[group(step)], basis.at[:, :, home], send.at[step], recv.at[step],
            group(step), slab,
        )

    def give_start(step, carry):
        give(step).start()
        return carry

    def give_wait(step, carry):
        give(step).wait()
        return carry

    lax.fori_loop(1, 8, give_start, 0)
    basis[:, :, home] = blocks[mine]
    r_rows[...] = upper_all[pl.ds(pl.multiple_of(64 * mine, 64), 64), :]
    lax.fori_loop(1, 8, give_wait, 0)


def everything(offsets, probes, coupling, viscosity, weight):
    comps, columns, cells = probes.shape
    tiles = cells // 128
    unknowns = 3 * cells * lax.axis_size("slab")
    dma = lambda count: pltpu.SemaphoreType.DMA((count,))
    vmem = lambda *shape: pltpu.VMEM(shape, jnp.float32)
    return pl.pallas_call(
        functools.partial(whole_kernel, 1.0 / unknowns),
        out_shape=(struct(comps, columns, cells), struct(64, 512)),
        in_specs=[pl.BlockSpec(memory_space=pltpu.SMEM)] + [HBM] * 4,
        out_specs=(VMEM, VMEM),
        scratch_shapes=[
            vmem(comps, 8, columns, 128),
            vmem(2, 16, 5, 8, 128),
            vmem(512, 896),
            vmem(512, 512),
            vmem(8, 3, 64, 128),
            vmem(comps, columns, cells),
            vmem(3, 3, BANDS, cells),
            vmem(1, cells),
            vmem(3, cells),
            vmem(comps, columns, 128),
            vmem(comps, columns, 128),
            vmem(3, 3, BANDS, 128),
            vmem(3, 3, BANDS, 128),
            vmem(1, 128),
            vmem(1, 128),
            vmem(3, 128),
            vmem(3, 128),
            vmem(tiles + 1, 9 * BANDS + 3, 8, 128),
            vmem(tiles, comps, columns, 128),
            vmem(2, 16, 5, 8, 128),
            vmem(16, 5, 8, 128),
            vmem(16, 5, 8, 128),
            vmem(16, 5, 8, 128),
            vmem(5, 8, 128),
            vmem(4, 5, 8, 128),
            vmem(5, 8, 128),
            vmem(4, 5, 8, 128),
            vmem(5, 8, 128),
        ]
        + [dma(8)] * 4
        + [dma(16)] * 4
        + [dma(4)] * 4
        + [dma(16)] * 4
        + [dma(4), dma(8), dma(8)],
        compiler_params=pltpu.CompilerParams(
            collective_id=0, has_side_effects=True, vmem_limit_bytes=61 * 1024 * 1024
        ),
        name="everything",
    )(offsets, probes, coupling, viscosity, weight)


def place_kernel(basis, r_rows, basis_out, r_out):
    basis_out[...] = basis[...]
    r_out[...] = r_rows[...]


def placed(basis, r_rows):
    return pl.pallas_call(
        place_kernel,
        out_shape=(struct(*basis.shape), struct(*r_rows.shape)),
        in_specs=[VMEM, VMEM],
        out_specs=(VMEM, VMEM),
        compiler_params=pltpu.CompilerParams(vmem_limit_bytes=4 * 1024 * 1024),
        name="placed",
    )(basis, r_rows)


def body(probes, viscosity, coupling, misfit_weight, band_offsets):
    return placed(
        *everything(
            band_offsets, probes, coupling.transpose(1, 2, 0, 3), viscosity[None, :], misfit_weight
        )
    )


def solution(mesh):
    return jax.shard_map(
        body,
        mesh=mesh,
        in_specs=(
            P(None, "probe", "slab"),
            P("slab"),
            P(None, None, None, "slab"),
            P(None, "slab"),
            P(),
        ),
        out_specs=(P(None, "probe", "slab"), P("probe", None)),
        check_vma=False,
    )
```

```python
import functools

import jax
import jax.numpy as jnp
from jax import lax
from jax.experimental import pallas as pl
from jax.experimental.pallas import tpu as pltpu
from jax.sharding import PartitionSpec as P

BANDS = 4
HIGHEST = lax.Precision.HIGHEST
VMEM = pl.BlockSpec(memory_space=pltpu.VMEM)
HBM = pl.BlockSpec(memory_space=pltpu.HBM)
LIMIT = 48 * 1024 * 1024


def struct(*shape):
    return jax.ShapeDtypeStruct(shape, jnp.float32)


def put(source, target, send, recv, probe, slab):
    return pltpu.make_async_remote_copy(
        src_ref=source,
        dst_ref=target,
        send_sem=send,
        recv_sem=recv,
        device_id=(probe, slab),
        device_id_type=pl.DeviceIdType.MESH,
    )


def greet(barrier, probe, slab):
    pl.semaphore_signal(
        barrier, inc=1, device_id=(probe, slab), device_id_type=pl.DeviceIdType.MESH
    )


SIDE_CHUNKS = [(row, lane) for row in range(8) for lane in range(row // 2, 4)]


def tile_place(tile):
    return tile // 80, tile % 80 // 5, tile % 5


def spread_row(value, row):
    return jnp.broadcast_to(value[row : row + 1, :], value.shape)


def eliminate(block, base, meanwhile):
    rows = lax.broadcasted_iota(jnp.int32, (8, 128), 0)
    work = [block[8 * i : 8 * i + 8] for i in range(8)]

    def spread_columns(i, turn):
        at = base + 8 * turn
        return [jnp.broadcast_to(work[i][:, at + s : at + s + 1], (8, 128)) for s in range(8)]

    own = spread_columns(0, 0)
    for turn in range(8):
        columns = {i: spread_columns(i, turn) for i in range(turn + 1, 8)}
        columns[turn] = own
        following = {i: spread_columns(i, turn + 1) for i in (turn, turn + 1) if turn < 7}
        pivots = jnp.ones((8, 128), jnp.float32)
        for s in range(8):
            pivot = spread_row(columns[turn][s], s)
            inverse = 1.0 / pivot
            pivots = jnp.where(rows == s, pivot, pivots)
            lead = spread_row(work[turn], s)
            leads = {q: spread_row(columns[turn][q], s) for q in range(s + 1, 8)}
            beyond = [spread_row(value, s) for value in following.get(turn, [])]
            for i in range(turn, 8):
                ratio = columns[i][s] * inverse
                if i == turn:
                    ratio = jnp.where(rows > s, ratio, 0.0)
                work[i] = work[i] - ratio * lead
                for q in range(s + 1, 8):
                    columns[i][q] = columns[i][q] - ratio * leads[q]
                if i in following:
                    following[i] = [
                        value - ratio * top for value, top in zip(following[i], beyond)
                    ]
        work[turn] = work[turn] * lax.rsqrt(pivots)
        own = following.get(turn + 1)
        count = len(meanwhile)
        for item in meanwhile[count * turn // 8 : count * (turn + 1) // 8]:
            item()
    return jnp.concatenate(work, 0)


def product(left, right, dims):
    return lax.dot_general(
        left, right, (dims, ((), ())), precision=HIGHEST, preferred_element_type=jnp.float32
    )


def factorize(work, upper_all, blocks):
    size, width = 512, 896
    lanes = lax.broadcasted_iota(jnp.int32, (64, 128), 1)
    rows = lax.broadcasted_iota(jnp.int32, (64, 128), 0)
    block = work[0:64, 0:128]
    meanwhile = []
    for step in range(8):
        lo, hi = 64 * step, 64 * step + 64
        base = 64 * (step % 2)
        tile = 128 * (step // 2)
        own = jnp.logical_and(lanes >= base, lanes < base + 64)
        unit = (lanes == rows + (64 - base)).astype(jnp.float32)
        done = eliminate(jnp.where(own, block, unit), base, meanwhile)
        triangle = jnp.where(jnp.logical_and(own, lanes - base >= rows), done, 0.0)
        left = jnp.where(own, 0.0, done)
        start = 128 * (hi // 128)

        def upper_of(at, count, lo=lo, hi=hi, left=left):
            strip = work[lo:hi, at : at + count]
            return product(left, jnp.concatenate([strip, strip], 0), ((1,), (0,)))

        if hi == size:
            upper_all[lo:hi, tile : tile + 128] = triangle
            last = upper_of(size, 384)
            for comp in range(3):
                blocks[step, comp] = last[:, 128 * comp : 128 * comp + 128]
            break
        first = upper_of(start, 128)
        trail = product(first, first, ((0,), (0,)))
        block = work[hi : hi + 64, start : start + 128] - trail[hi - start : hi - start + 64]
        upper = {start: first}
        meanwhile = []
        spans = [(at, min(256, size - at)) for at in range(start + 128, size, 256)]
        spans += [(size, 256), (size + 256, 128)]

        def keep(lo=lo, hi=hi, base=base, tile=tile, own=own, triangle=triangle, first=first, start=start):
            if base == 0:
                upper_all[lo:hi, tile : tile + 128] = jnp.where(own, triangle, first)
            else:
                upper_all[lo:hi, tile : tile + 128] = triangle
                upper_all[lo:hi, start : start + 128] = first

        def solve(at, count, step=step, lo=lo, hi=hi, upper=upper, upper_of=upper_of):
            value = upper_of(at, count)
            for part in range(at, at + count, 128):
                piece = value[:, part - at : part - at + 128]
                upper[part] = piece
                if part < size:
                    upper_all[lo:hi, part : part + 128] = piece
                else:
                    blocks[step, (part - size) // 128] = piece

        def update(at, count, hi=hi, start=start, upper=upper):
            reach = min(size, at + count)
            left_side = jnp.concatenate([upper[part] for part in range(start, reach, 128)], 1)
            right_side = jnp.concatenate([upper[part] for part in range(at, at + count, 128)], 1)
            trail = product(left_side, right_side, ((0,), (0,)))
            work[hi:reach, at : at + count] = work[hi:reach, at : at + count] - trail[hi - start :]

        meanwhile.append(keep)
        solves = [functools.partial(solve, at, count) for at, count in spans]
        updates = [functools.partial(update, at, count) for at, count in spans]
        if base:
            def below(hi=hi, start=start, trail=trail):
                work[hi + 64 : start + 128, start : start + 128] = (
                    work[hi + 64 : start + 128, start : start + 128] - trail[hi + 64 - start :]
                )
            meanwhile.append(below)
        if base:
            def beside(hi=hi, start=start, block=block):
                work[hi : hi + 64, start : start + 128] = block
            meanwhile.append(beside)
        meanwhile += solves + updates


def whole_kernel(
    scale,
    offsets, probes_in, coupling_in, viscosity_in, weight_in, basis, r_rows,
    field, gram, work, upper_all, blocks, probes, coupling, viscosity, weight, low, high, coup_low, coup_high, visc_low, visc_high, weight_low, weight_high,
    spread, panel, part, half_in, half, plane_in, piece, near_in, near, line_in, total,
    halo_s, halo_r, swap_s, swap_r, core_s, core_r, fold_s, fold_r,
    near_s, near_r, line_s, line_r, back_s, back_r, pair_s, pair_r, load, send, recv,
):
    loads = [
        pltpu.make_async_copy(coupling_in, coupling, load.at[0]),
        pltpu.make_async_copy(viscosity_in, viscosity, load.at[1]),
        pltpu.make_async_copy(weight_in, weight, load.at[2]),
        pltpu.make_async_copy(probes_in, probes, load.at[3]),
    ]
    for copy in loads:
        copy.start()
    mine, slab = lax.axis_index("probe"), lax.axis_index("slab")
    count = lax.axis_size("slab")
    after, before = lax.rem(slab + 1, count), lax.rem(slab + count - 1, count)
    core, chip = lax.rem(slab, 2), slab // 2
    side, place = chip // 16, lax.rem(chip, 16)
    twin = slab + 1 - 2 * core
    rank = side * 8 + mine
    cells = probes.shape[2]
    tiles = cells // 128
    ring = tiles + 1

    def group(step):
        return lax.rem(mine + step, 8)

    def plane_rank(step):
        return lax.rem(rank + step, 16)

    def in_plane(step):
        other = plane_rank(step)
        return lax.rem(other, 8), 32 * (other // 8) + 2 * place + core

    quad, spot = place // 4, lax.rem(place, 4)

    def in_quad(step):
        return mine, 32 * side + 2 * (4 * quad + lax.rem(spot + step, 4)) + core

    def in_line(step):
        return mine, 32 * side + 2 * (4 * lax.rem(quad + step, 4) + spot) + core

    barrier = pltpu.get_barrier_semaphore()
    greet(barrier, mine, after)
    greet(barrier, mine, before)

    def greet_plane(step, carry):
        greet(barrier, *in_plane(step))
        return carry

    def greet_line(step, carry):
        greet(barrier, *in_quad(step))
        greet(barrier, *in_line(step))
        return carry

    lax.fori_loop(1, 4, greet_line, 0)
    lax.fori_loop(1, 16, greet_plane, 0)
    pl.semaphore_wait(barrier, 23)

    edge = pl.ds(cells - 128, 128)
    start = pl.ds(0, 128)
    copies = [
        put(probes_in.at[:, :, edge], low, halo_s.at[0], halo_r.at[0], mine, after),
        put(probes_in.at[:, :, start], high, halo_s.at[1], halo_r.at[1], mine, before),
        put(coupling_in.at[:, :, :, edge], coup_low, halo_s.at[2], halo_r.at[2], mine, after),
        put(coupling_in.at[:, :, :, start], coup_high, halo_s.at[3], halo_r.at[3], mine, before),
        put(viscosity_in.at[:, edge], visc_low, halo_s.at[4], halo_r.at[4], mine, after),
        put(viscosity_in.at[:, start], visc_high, halo_s.at[5], halo_r.at[5], mine, before),
        put(weight_in.at[:, edge], weight_low, halo_s.at[6], halo_r.at[6], mine, after),
        put(weight_in.at[:, start], weight_high, halo_s.at[7], halo_r.at[7], mine, before),
    ]
    for copy in copies:
        copy.start()

    lanes = lax.broadcasted_iota(jnp.int32, (8, 128), 1)
    from_high = lanes < 64
    inside = jnp.logical_or(
        jnp.logical_and(from_high, slab < count - 1),
        jnp.logical_and(jnp.logical_not(from_high), slab > 0),
    )

    def wide(value):
        return jnp.broadcast_to(value, (8, 128))

    def fill(tile, coup, visc, wt):
        for band in range(BANDS):
            for comp in range(3):
                for source in range(3):
                    spread[tile, 9 * band + 3 * comp + source] = coup(comp, source, band)
        for comp in range(3):
            spread[tile, 36 + comp] = visc * (wt(comp) * visc)

    for copy in loads:
        copy.wait()
    for tile in range(tiles):
        at = slice(128 * tile, 128 * tile + 128)
        fill(
            tile,
            lambda comp, source, band: wide(coupling[comp, source, band : band + 1, at]),
            wide(viscosity[:, at]),
            lambda comp: wide(weight[comp : comp + 1, at]),
        )
    for copy in copies:
        copy.wait()

    def merged(below, above):
        return jnp.where(inside, jnp.where(from_high, wide(above), wide(below)), 0.0)

    fill(
        tiles,
        lambda comp, source, band: merged(
            coup_low[comp, source, band : band + 1], coup_high[comp, source, band : band + 1]
        ),
        merged(visc_low[...], visc_high[...]),
        lambda comp: merged(weight_low[comp : comp + 1], weight_high[comp : comp + 1]),
    )

    def shifted(values, offset):
        turned = [pltpu.roll(value, lax.rem(128 - offset, 128), 1) for value in values]
        reach = lanes + offset
        past, ahead = reach > 127, reach < 0
        return [
            jnp.where(
                past,
                turned[(tile + 1) % ring],
                jnp.where(ahead, turned[(tile + ring - 1) % ring], turned[tile]),
            )
            for tile in range(ring)
        ]

    def swap(step, rows):
        return put(
            panel.at[group(step), :, rows, :], field.at[:, mine, rows, :],
            swap_s.at[step], swap_r.at[step], group(step), slab,
        )

    def probe_rows(at, carry):
        rows = pl.ds(pl.multiple_of(8 * at, 8), 8)
        values = []
        for comp in range(3):
            own = [probes[comp, rows, 128 * tile : 128 * tile + 128] for tile in range(tiles)]
            ends = jnp.where(from_high, high[comp, rows, :], low[comp, rows, :])
            values.append(own + [jnp.where(inside, ends, 0.0)])
        for turn in range(2):
            result = [list(value) for value in values]
            for band in range(BANDS):
                moved = [shifted(value, offsets[band]) for value in values]
                for comp in range(3):
                    for source in range(3):
                        for tile in range(ring):
                            coef = spread[tile, 9 * band + 3 * comp + source]
                            result[comp][tile] = result[comp][tile] + coef * moved[source][tile]
            scaled = [
                [spread[tile, 36 + comp] * result[comp][tile] for tile in range(ring)]
                for comp in range(3)
            ]
            values = [list(value) for value in scaled]
            for band in range(BANDS):
                for source in range(3):
                    parts = []
                    for tile in range(ring):
                        term = spread[tile, 9 * band + source] * scaled[0][tile]
                        term = term + spread[tile, 9 * band + 3 + source] * scaled[1][tile]
                        term = term + spread[tile, 9 * band + 6 + source] * scaled[2][tile]
                        parts.append(term)
                    moved = shifted(parts, -offsets[band])
                    for tile in range(ring):
                        values[source][tile] = values[source][tile] + moved[tile]
            if turn == 0:
                for comp in range(3):
                    values[comp][tiles] = jnp.where(inside, values[comp][tiles], 0.0)
        for comp in range(3):
            for tile in range(tiles):
                panel[tile, comp, rows, :] = values[comp][tile]

        return carry

    def two_rows(at, carry):
        lax.fori_loop(2 * at, 2 * at + 2, probe_rows, 0)
        rows = pl.ds(pl.multiple_of(16 * at, 16), 16)

        def send(step, inner):
            swap(step, rows).start()
            return inner

        lax.fori_loop(1, 8, send, 0)
        return carry

    lax.fori_loop(0, probes.shape[1] // 16, two_rows, 0)
    field[:, mine] = panel[mine]
    every = pl.ds(0, probes.shape[1])

    def swap_wait(step, carry):
        swap(step, every).wait()
        return carry

    lax.fori_loop(1, 8, swap_wait, 0)

    whole = jnp.concatenate([field[comp].reshape(512, 128) for comp in range(3)], 1)
    products = [
        lax.dot_general(
            whole[: 128 * lane + 128], whole[128 * lane : 128 * lane + 128],
            (((1,), (1,)), ((), ())), precision=HIGHEST, preferred_element_type=jnp.float32,
        )
        for lane in range(4)
    ]
    for chunk, (row, lane) in enumerate(SIDE_CHUNKS):
        for i in range(8):
            at = 64 * row + 8 * i
            part[tile_place(8 * chunk + i)] = products[lane][at : at + 8]

    def to_twin(step):
        other = plane_rank(step)
        return put(
            part.at[1 - core, other], half_in.at[other], core_s.at[step], core_r.at[step],
            mine, twin,
        )

    def fold(step):
        return put(
            half.at[plane_rank(step)], plane_in.at[rank], fold_s.at[step], fold_r.at[step],
            *in_plane(step),
        )

    def twin_start(step, carry):
        to_twin(lax.rem(step, 16)).start()
        return carry

    def add_twin(step):
        other = plane_rank(step)
        to_twin(step).wait()
        half[other] = part[core, other] + half_in[other]

    def twin_wait(step, carry):
        add_twin(step)
        fold(step).start()
        return carry

    lax.fori_loop(1, 17, twin_start, 0)
    lax.fori_loop(1, 16, twin_wait, 0)
    add_twin(0)
    plane_in[rank] = half[rank]

    def fold_wait(step, carry):
        fold(step).wait()
        return carry

    lax.fori_loop(1, 16, fold_wait, 0)
    summed = plane_in[0]
    for other in range(1, 16):
        summed = summed + plane_in[other]
    piece[...] = summed

    def close_by(step):
        return put(
            piece, near_in.at[spot], near_s.at[step], near_r.at[step], *in_quad(step)
        )

    def line(step):
        return put(
            near, line_in.at[quad], line_s.at[step], line_r.at[step], *in_line(step)
        )

    for step in range(1, 4):
        close_by(step).start()
    near_in[spot] = summed
    for step in range(1, 4):
        close_by(step).wait()
    summed = near_in[0] + near_in[1] + near_in[2] + near_in[3]
    near[...] = summed
    for step in range(1, 4):
        line(step).start()
    line_in[quad] = summed
    for step in range(1, 4):
        line(step).wait()
    summed = line_in[0] + line_in[1] + line_in[2] + line_in[3]
    total[...] = summed

    def back(step):
        return put(
            total, gram.at[core, rank], back_s.at[step], back_r.at[step], *in_plane(step)
        )

    def pair(step):
        other = lax.rem(rank + 16 - step, 16)
        return put(
            gram.at[core, other], gram.at[core, other], pair_s.at[step], pair_r.at[step],
            mine, twin,
        )

    def back_start(step, carry):
        back(step).start()
        return carry

    lax.fori_loop(1, 16, back_start, 0)
    size = 512
    for comp in range(3):
        work[:, size + 128 * comp : size + 128 * comp + 128] = field[comp].reshape(size, 128)
    upper_all[...] = jnp.zeros_like(upper_all)
    gram[core, rank] = summed
    pair(0).start()

    def back_wait(step, carry):
        back(step).wait()
        pair(step).start()
        return carry

    lax.fori_loop(1, 16, back_wait, 0)

    def pair_wait(step, carry):
        pair(step).wait()
        return carry

    lax.fori_loop(0, 16, pair_wait, 0)

    for chunk, (row, lane) in enumerate(SIDE_CHUNKS):
        for i in range(8):
            at = 64 * row + 8 * i
            work[at : at + 8, 128 * lane : 128 * lane + 128] = (
                gram[tile_place(8 * chunk + i)] * scale
            )
    factorize(work, upper_all, blocks)

    home = pl.ds(pl.multiple_of(128 * mine, 128), 128)

    def give(step):
        return put(
            blocks.at[group(step)], basis.at[:, :, home], send.at[step], recv.at[step],
            group(step), slab,
        )

    def give_start(step, carry):
        give(step).start()
        return carry

    def give_wait(step, carry):
        give(step).wait()
        return carry

    lax.fori_loop(1, 8, give_start, 0)
    keep_own = pltpu.make_async_copy(blocks.at[mine], basis.at[:, :, home], load.at[4])
    keep_own.start()
    r_rows[...] = upper_all[pl.ds(pl.multiple_of(64 * mine, 64), 64), :]
    lax.fori_loop(1, 8, give_wait, 0)
    keep_own.wait()


def everything(offsets, probes, coupling, viscosity, weight):
    comps, columns, cells = probes.shape
    tiles = cells // 128
    unknowns = 3 * cells * lax.axis_size("slab")
    dma = lambda count: pltpu.SemaphoreType.DMA((count,))
    vmem = lambda *shape: pltpu.VMEM(shape, jnp.float32)
    return pl.pallas_call(
        functools.partial(whole_kernel, 1.0 / unknowns),
        out_shape=(struct(comps, columns, cells), struct(64, 512)),
        in_specs=[pl.BlockSpec(memory_space=pltpu.SMEM)] + [HBM] * 4,
        out_specs=(HBM, VMEM),
        scratch_shapes=[
            vmem(comps, 8, columns, 128),
            vmem(2, 16, 5, 8, 128),
            vmem(512, 896),
            vmem(512, 512),
            vmem(8, 3, 64, 128),
            vmem(comps, columns, cells),
            vmem(3, 3, BANDS, cells),
            vmem(1, cells),
            vmem(3, cells),
            vmem(comps, columns, 128),
            vmem(comps, columns, 128),
            vmem(3, 3, BANDS, 128),
            vmem(3, 3, BANDS, 128),
            vmem(1, 128),
            vmem(1, 128),
            vmem(3, 128),
            vmem(3, 128),
            vmem(tiles + 1, 9 * BANDS + 3, 8, 128),
            vmem(tiles, comps, columns, 128),
            vmem(2, 16, 5, 8, 128),
            vmem(16, 5, 8, 128),
            vmem(16, 5, 8, 128),
            vmem(16, 5, 8, 128),
            vmem(5, 8, 128),
            vmem(4, 5, 8, 128),
            vmem(5, 8, 128),
            vmem(4, 5, 8, 128),
            vmem(5, 8, 128),
        ]
        + [dma(8)] * 4
        + [dma(16)] * 4
        + [dma(4)] * 4
        + [dma(16)] * 4
        + [dma(5), dma(8), dma(8)],
        compiler_params=pltpu.CompilerParams(
            collective_id=0, has_side_effects=True, vmem_limit_bytes=61 * 1024 * 1024
        ),
        name="everything",
    )(offsets, probes, coupling, viscosity, weight)


def place_kernel(basis, r_rows, basis_out, r_out):
    basis_out[...] = basis[...]
    r_out[...] = r_rows[...]


def placed(basis, r_rows):
    return pl.pallas_call(
        place_kernel,
        out_shape=(struct(*basis.shape), struct(*r_rows.shape)),
        in_specs=[VMEM, VMEM],
        out_specs=(VMEM, VMEM),
        compiler_params=pltpu.CompilerParams(vmem_limit_bytes=63 * 1024 * 1024),
        name="placed",
    )(basis, r_rows)


def body(probes, viscosity, coupling, misfit_weight, band_offsets):
    return placed(
        *everything(
            band_offsets, probes, coupling.transpose(1, 2, 0, 3), viscosity[None, :], misfit_weight
        )
    )


def solution(mesh):
    return jax.shard_map(
        body,
        mesh=mesh,
        in_specs=(
            P(None, "probe", "slab"),
            P("slab"),
            P(None, None, None, "slab"),
            P(None, "slab"),
            P(),
        ),
        out_specs=(P(None, "probe", "slab"), P("probe", None)),
        check_vma=False,
    )
```

```python
import functools

import jax
import jax.numpy as jnp
from jax import lax
from jax.experimental import pallas as pl
from jax.experimental.pallas import tpu as pltpu
from jax.sharding import PartitionSpec as P

BANDS = 4
HIGHEST = lax.Precision.HIGHEST
VMEM = pl.BlockSpec(memory_space=pltpu.VMEM)
HBM = pl.BlockSpec(memory_space=pltpu.HBM)
LIMIT = 48 * 1024 * 1024


def struct(*shape):
    return jax.ShapeDtypeStruct(shape, jnp.float32)


def put(source, target, send, recv, probe, slab):
    return pltpu.make_async_remote_copy(
        src_ref=source,
        dst_ref=target,
        send_sem=send,
        recv_sem=recv,
        device_id=(probe, slab),
        device_id_type=pl.DeviceIdType.MESH,
    )


def greet(barrier, probe, slab):
    pl.semaphore_signal(
        barrier, inc=1, device_id=(probe, slab), device_id_type=pl.DeviceIdType.MESH
    )


SIDE_CHUNKS = [(row, lane) for row in range(8) for lane in range(row // 2, 4)]


def tile_place(tile):
    return tile // 80, tile % 80 // 5, tile % 5


def spread_row(value, row):
    return jnp.broadcast_to(value[row : row + 1, :], value.shape)


def eliminate(block, base, meanwhile):
    rows = lax.broadcasted_iota(jnp.int32, (8, 128), 0)
    work = [block[8 * i : 8 * i + 8] for i in range(8)]

    def spread_columns(i, turn):
        at = base + 8 * turn
        return [jnp.broadcast_to(work[i][:, at + s : at + s + 1], (8, 128)) for s in range(8)]

    own = spread_columns(0, 0)
    for turn in range(8):
        columns = {i: spread_columns(i, turn) for i in range(turn + 1, 8)}
        columns[turn] = own
        following = {i: spread_columns(i, turn + 1) for i in (turn, turn + 1) if turn < 7}
        pivots = jnp.ones((8, 128), jnp.float32)
        for s in range(8):
            pivot = spread_row(columns[turn][s], s)
            inverse = 1.0 / pivot
            pivots = jnp.where(rows == s, pivot, pivots)
            lead = spread_row(work[turn], s)
            leads = {q: spread_row(columns[turn][q], s) for q in range(s + 1, 8)}
            beyond = [spread_row(value, s) for value in following.get(turn, [])]
            for i in range(turn, 8):
                ratio = columns[i][s] * inverse
                if i == turn:
                    ratio = jnp.where(rows > s, ratio, 0.0)
                work[i] = work[i] - ratio * lead
                for q in range(s + 1, 8):
                    columns[i][q] = columns[i][q] - ratio * leads[q]
                if i in following:
                    following[i] = [
                        value - ratio * top for value, top in zip(following[i], beyond)
                    ]
        work[turn] = work[turn] * lax.rsqrt(pivots)
        own = following.get(turn + 1)
        count = len(meanwhile)
        for item in meanwhile[count * turn // 8 : count * (turn + 1) // 8]:
            item()
    return jnp.concatenate(work, 0)


def product(left, right, dims):
    return lax.dot_general(
        left, right, (dims, ((), ())), precision=HIGHEST, preferred_element_type=jnp.float32
    )


def factorize(work, upper_all, blocks):
    size, width = 512, 896
    lanes = lax.broadcasted_iota(jnp.int32, (64, 128), 1)
    rows = lax.broadcasted_iota(jnp.int32, (64, 128), 0)
    block = work[0:64, 0:128]
    meanwhile = []
    for step in range(8):
        lo, hi = 64 * step, 64 * step + 64
        base = 64 * (step % 2)
        tile = 128 * (step // 2)
        own = jnp.logical_and(lanes >= base, lanes < base + 64)
        unit = (lanes == rows + (64 - base)).astype(jnp.float32)
        done = eliminate(jnp.where(own, block, unit), base, meanwhile)
        triangle = jnp.where(jnp.logical_and(own, lanes - base >= rows), done, 0.0)
        left = jnp.where(own, 0.0, done)
        start = 128 * (hi // 128)

        def upper_of(at, count, lo=lo, hi=hi, left=left):
            strip = work[lo:hi, at : at + count]
            return product(left, jnp.concatenate([strip, strip], 0), ((1,), (0,)))

        if hi == size:
            upper_all[lo:hi, tile : tile + 128] = triangle
            last = upper_of(size, 384)
            for comp in range(3):
                blocks[step, comp] = last[:, 128 * comp : 128 * comp + 128]
            break
        first = upper_of(start, 128)
        trail = product(first, first, ((0,), (0,)))
        block = work[hi : hi + 64, start : start + 128] - trail[hi - start : hi - start + 64]
        upper = {start: first}
        meanwhile = []
        spans = [(at, min(256, size - at)) for at in range(start + 128, size, 256)]
        spans += [(size, 256), (size + 256, 128)]

        def keep(lo=lo, hi=hi, base=base, tile=tile, own=own, triangle=triangle, first=first, start=start):
            if base == 0:
                upper_all[lo:hi, tile : tile + 128] = jnp.where(own, triangle, first)
            else:
                upper_all[lo:hi, tile : tile + 128] = triangle
                upper_all[lo:hi, start : start + 128] = first

        def solve(at, count, step=step, lo=lo, hi=hi, upper=upper, upper_of=upper_of):
            value = upper_of(at, count)
            for part in range(at, at + count, 128):
                piece = value[:, part - at : part - at + 128]
                upper[part] = piece
                if part < size:
                    upper_all[lo:hi, part : part + 128] = piece
                else:
                    blocks[step, (part - size) // 128] = piece

        def update(at, count, hi=hi, start=start, upper=upper):
            reach = min(size, at + count)
            left_side = jnp.concatenate([upper[part] for part in range(start, reach, 128)], 1)
            right_side = jnp.concatenate([upper[part] for part in range(at, at + count, 128)], 1)
            trail = product(left_side, right_side, ((0,), (0,)))
            work[hi:reach, at : at + count] = work[hi:reach, at : at + count] - trail[hi - start :]

        meanwhile.append(keep)
        solves = [functools.partial(solve, at, count) for at, count in spans]
        updates = [functools.partial(update, at, count) for at, count in spans]
        if base:
            def below(hi=hi, start=start, trail=trail):
                work[hi + 64 : start + 128, start : start + 128] = (
                    work[hi + 64 : start + 128, start : start + 128] - trail[hi + 64 - start :]
                )
            meanwhile.append(below)
        if base:
            def beside(hi=hi, start=start, block=block):
                work[hi : hi + 64, start : start + 128] = block
            meanwhile.append(beside)
        meanwhile += solves + updates


def whole_kernel(
    scale,
    offsets, probes_in, coupling_in, viscosity_in, weight_in, basis, r_rows,
    field, gram, work, upper_all, blocks, probes, coupling, viscosity, weight, low, high, coup_low, coup_high, visc_low, visc_high, weight_low, weight_high,
    spread, panel, part, half_in, half, plane_in, piece, near_in, near, line_in, total,
    halo_s, halo_r, swap_s, swap_r, core_s, core_r, fold_s, fold_r,
    near_s, near_r, line_s, line_r, back_s, back_r, pair_s, pair_r, load, send, recv,
):
    loads = [
        pltpu.make_async_copy(coupling_in, coupling, load.at[0]),
        pltpu.make_async_copy(viscosity_in, viscosity, load.at[1]),
        pltpu.make_async_copy(weight_in, weight, load.at[2]),
        pltpu.make_async_copy(probes_in, probes, load.at[3]),
    ]
    for copy in loads:
        copy.start()
    mine, slab = lax.axis_index("probe"), lax.axis_index("slab")
    count = lax.axis_size("slab")
    after, before = lax.rem(slab + 1, count), lax.rem(slab + count - 1, count)
    core, chip = lax.rem(slab, 2), slab // 2
    side, place = chip // 16, lax.rem(chip, 16)
    twin = slab + 1 - 2 * core
    rank = side * 8 + mine
    cells = probes.shape[2]
    tiles = cells // 128
    ring = tiles + 1

    def group(step):
        return lax.rem(mine + step, 8)

    def plane_rank(step):
        return lax.rem(rank + step, 16)

    def in_plane(step):
        other = plane_rank(step)
        return lax.rem(other, 8), 32 * (other // 8) + 2 * place + core

    quad, spot = place // 4, lax.rem(place, 4)

    def in_quad(step):
        return mine, 32 * side + 2 * (4 * quad + lax.rem(spot + step, 4)) + core

    def in_line(step):
        return mine, 32 * side + 2 * (4 * lax.rem(quad + step, 4) + spot) + core

    barrier = pltpu.get_barrier_semaphore()
    greet(barrier, mine, after)
    greet(barrier, mine, before)

    def greet_plane(step, carry):
        greet(barrier, *in_plane(step))
        return carry

    def greet_line(step, carry):
        greet(barrier, *in_quad(step))
        greet(barrier, *in_line(step))
        return carry

    lax.fori_loop(1, 4, greet_line, 0)
    lax.fori_loop(1, 16, greet_plane, 0)
    pl.semaphore_wait(barrier, 23)

    edge = pl.ds(cells - 128, 128)
    start = pl.ds(0, 128)
    copies = [
        put(probes_in.at[:, :, edge], low, halo_s.at[0], halo_r.at[0], mine, after),
        put(probes_in.at[:, :, start], high, halo_s.at[1], halo_r.at[1], mine, before),
        put(coupling_in.at[:, :, :, edge], coup_low, halo_s.at[2], halo_r.at[2], mine, after),
        put(coupling_in.at[:, :, :, start], coup_high, halo_s.at[3], halo_r.at[3], mine, before),
        put(viscosity_in.at[:, edge], visc_low, halo_s.at[4], halo_r.at[4], mine, after),
        put(viscosity_in.at[:, start], visc_high, halo_s.at[5], halo_r.at[5], mine, before),
        put(weight_in.at[:, edge], weight_low, halo_s.at[6], halo_r.at[6], mine, after),
        put(weight_in.at[:, start], weight_high, halo_s.at[7], halo_r.at[7], mine, before),
    ]
    for copy in copies:
        copy.start()

    lanes = lax.broadcasted_iota(jnp.int32, (8, 128), 1)
    from_high = lanes < 64
    inside = jnp.logical_or(
        jnp.logical_and(from_high, slab < count - 1),
        jnp.logical_and(jnp.logical_not(from_high), slab > 0),
    )

    def wide(value):
        return jnp.broadcast_to(value, (8, 128))

    def fill(tile, coup, visc, wt):
        for band in range(BANDS):
            for comp in range(3):
                for source in range(3):
                    spread[tile, 9 * band + 3 * comp + source] = coup(comp, source, band)
        for comp in range(3):
            spread[tile, 36 + comp] = visc * (wt(comp) * visc)

    for copy in loads:
        copy.wait()
    for tile in range(tiles):
        at = slice(128 * tile, 128 * tile + 128)
        fill(
            tile,
            lambda comp, source, band: wide(coupling[comp, source, band : band + 1, at]),
            wide(viscosity[:, at]),
            lambda comp: wide(weight[comp : comp + 1, at]),
        )
    for copy in copies:
        copy.wait_recv()

    def merged(below, above):
        return jnp.where(inside, jnp.where(from_high, wide(above), wide(below)), 0.0)

    fill(
        tiles,
        lambda comp, source, band: merged(
            coup_low[comp, source, band : band + 1], coup_high[comp, source, band : band + 1]
        ),
        merged(visc_low[...], visc_high[...]),
        lambda comp: merged(weight_low[comp : comp + 1], weight_high[comp : comp + 1]),
    )

    def shifted(values, offset):
        turned = [pltpu.roll(value, lax.rem(128 - offset, 128), 1) for value in values]
        reach = lanes + offset
        past, ahead = reach > 127, reach < 0
        return [
            jnp.where(
                past,
                turned[(tile + 1) % ring],
                jnp.where(ahead, turned[(tile + ring - 1) % ring], turned[tile]),
            )
            for tile in range(ring)
        ]

    def swap(step, rows):
        return put(
            panel.at[group(step), :, rows, :], field.at[:, mine, rows, :],
            swap_s.at[step], swap_r.at[step], group(step), slab,
        )

    def probe_rows(at, carry):
        rows = pl.ds(pl.multiple_of(8 * at, 8), 8)
        values = []
        for comp in range(3):
            own = [probes[comp, rows, 128 * tile : 128 * tile + 128] for tile in range(tiles)]
            ends = jnp.where(from_high, high[comp, rows, :], low[comp, rows, :])
            values.append(own + [jnp.where(inside, ends, 0.0)])
        for turn in range(2):
            result = [list(value) for value in values]
            for band in range(BANDS):
                moved = [shifted(value, offsets[band]) for value in values]
                for comp in range(3):
                    for source in range(3):
                        for tile in range(ring):
                            coef = spread[tile, 9 * band + 3 * comp + source]
                            result[comp][tile] = result[comp][tile] + coef * moved[source][tile]
            scaled = [
                [spread[tile, 36 + comp] * result[comp][tile] for tile in range(ring)]
                for comp in range(3)
            ]
            values = [list(value) for value in scaled]
            for band in range(BANDS):
                for source in range(3):
                    parts = []
                    for tile in range(ring):
                        term = spread[tile, 9 * band + source] * scaled[0][tile]
                        term = term + spread[tile, 9 * band + 3 + source] * scaled[1][tile]
                        term = term + spread[tile, 9 * band + 6 + source] * scaled[2][tile]
                        parts.append(term)
                    moved = shifted(parts, -offsets[band])
                    for tile in range(ring):
                        values[source][tile] = values[source][tile] + moved[tile]
            if turn == 0:
                for comp in range(3):
                    values[comp][tiles] = jnp.where(inside, values[comp][tiles], 0.0)
        for comp in range(3):
            for tile in range(tiles):
                panel[tile, comp, rows, :] = values[comp][tile]

        return carry

    def two_rows(at, carry):
        lax.fori_loop(2 * at, 2 * at + 2, probe_rows, 0)
        rows = pl.ds(pl.multiple_of(16 * at, 16), 16)

        def send(step, inner):
            swap(step, rows).start()
            return inner

        lax.fori_loop(1, 8, send, 0)
        return carry

    lax.fori_loop(0, probes.shape[1] // 16, two_rows, 0)
    field[:, mine] = panel[mine]
    every = pl.ds(0, probes.shape[1])

    def swap_wait(step, carry):
        swap(step, every).wait_recv()
        return carry

    lax.fori_loop(1, 8, swap_wait, 0)

    whole = jnp.concatenate([field[comp].reshape(512, 128) for comp in range(3)], 1)
    products = [
        lax.dot_general(
            whole[: 128 * lane + 128], whole[128 * lane : 128 * lane + 128],
            (((1,), (1,)), ((), ())), precision=HIGHEST, preferred_element_type=jnp.float32,
        )
        for lane in range(4)
    ]
    for chunk, (row, lane) in enumerate(SIDE_CHUNKS):
        for i in range(8):
            at = 64 * row + 8 * i
            part[tile_place(8 * chunk + i)] = products[lane][at : at + 8]

    def to_twin(step):
        other = plane_rank(step)
        return put(
            part.at[1 - core, other], half_in.at[other], core_s.at[step], core_r.at[step],
            mine, twin,
        )

    def fold(step):
        return put(
            half.at[plane_rank(step)], plane_in.at[rank], fold_s.at[step], fold_r.at[step],
            *in_plane(step),
        )

    def twin_start(step, carry):
        to_twin(lax.rem(step, 16)).start()
        return carry

    def add_twin(step):
        other = plane_rank(step)
        to_twin(step).wait_recv()
        half[other] = part[core, other] + half_in[other]

    def twin_wait(step, carry):
        add_twin(step)
        fold(step).start()
        return carry

    lax.fori_loop(1, 17, twin_start, 0)
    lax.fori_loop(1, 16, twin_wait, 0)
    add_twin(0)
    plane_in[rank] = half[rank]

    def fold_wait(step, carry):
        fold(step).wait_recv()
        return carry

    lax.fori_loop(1, 16, fold_wait, 0)
    summed = plane_in[0]
    for other in range(1, 16):
        summed = summed + plane_in[other]
    piece[...] = summed

    def close_by(step):
        return put(
            piece, near_in.at[spot], near_s.at[step], near_r.at[step], *in_quad(step)
        )

    def line(step):
        return put(
            near, line_in.at[quad], line_s.at[step], line_r.at[step], *in_line(step)
        )

    for step in range(1, 4):
        close_by(step).start()
    near_in[spot] = summed
    for step in range(1, 4):
        close_by(step).wait_recv()
    summed = near_in[0] + near_in[1] + near_in[2] + near_in[3]
    near[...] = summed
    for step in range(1, 4):
        line(step).start()
    line_in[quad] = summed
    for step in range(1, 4):
        line(step).wait_recv()
    summed = line_in[0] + line_in[1] + line_in[2] + line_in[3]
    total[...] = summed

    def back(step):
        return put(
            total, gram.at[core, rank], back_s.at[step], back_r.at[step], *in_plane(step)
        )

    def pair(step):
        other = lax.rem(rank + 16 - step, 16)
        return put(
            gram.at[core, other], gram.at[core, other], pair_s.at[step], pair_r.at[step],
            mine, twin,
        )

    def back_start(step, carry):
        back(step).start()
        return carry

    lax.fori_loop(1, 16, back_start, 0)
    size = 512
    for comp in range(3):
        work[:, size + 128 * comp : size + 128 * comp + 128] = field[comp].reshape(size, 128)
    upper_all[...] = jnp.zeros_like(upper_all)
    gram[core, rank] = summed
    pair(0).start()

    def back_wait(step, carry):
        back(step).wait_recv()
        pair(step).start()
        return carry

    lax.fori_loop(1, 16, back_wait, 0)

    def pair_wait(step, carry):
        pair(step).wait_recv()
        return carry

    lax.fori_loop(0, 16, pair_wait, 0)

    for chunk, (row, lane) in enumerate(SIDE_CHUNKS):
        for i in range(8):
            at = 64 * row + 8 * i
            work[at : at + 8, 128 * lane : 128 * lane + 128] = (
                gram[tile_place(8 * chunk + i)] * scale
            )
    factorize(work, upper_all, blocks)

    home = pl.ds(pl.multiple_of(128 * mine, 128), 128)

    def give(step):
        return put(
            blocks.at[group(step)], basis.at[:, :, home], send.at[step], recv.at[step],
            group(step), slab,
        )

    def give_start(step, carry):
        give(step).start()
        return carry

    def give_wait(step, carry):
        give(step).wait()
        return carry

    lax.fori_loop(1, 8, give_start, 0)
    keep_own = pltpu.make_async_copy(blocks.at[mine], basis.at[:, :, home], load.at[4])
    keep_own.start()
    r_rows[...] = upper_all[pl.ds(pl.multiple_of(64 * mine, 64), 64), :]
    lax.fori_loop(1, 8, give_wait, 0)
    keep_own.wait()

    def left_group(step, carry):
        swap(step, every).wait_send()
        return carry

    def left_plane(step, carry):
        to_twin(step).wait_send()
        fold(step).wait_send()
        back(step).wait_send()
        pair(step).wait_send()
        return carry

    for copy in copies:
        copy.wait_send()
    lax.fori_loop(1, 8, left_group, 0)
    lax.fori_loop(1, 16, left_plane, 0)
    to_twin(0).wait_send()
    pair(0).wait_send()
    for step in range(1, 4):
        close_by(step).wait_send()
        line(step).wait_send()


def everything(offsets, probes, coupling, viscosity, weight):
    comps, columns, cells = probes.shape
    tiles = cells // 128
    unknowns = 3 * cells * lax.axis_size("slab")
    dma = lambda count: pltpu.SemaphoreType.DMA((count,))
    vmem = lambda *shape: pltpu.VMEM(shape, jnp.float32)
    return pl.pallas_call(
        functools.partial(whole_kernel, 1.0 / unknowns),
        out_shape=(struct(comps, columns, cells), struct(64, 512)),
        in_specs=[pl.BlockSpec(memory_space=pltpu.SMEM)] + [HBM] * 4,
        out_specs=(HBM, VMEM),
        scratch_shapes=[
            vmem(comps, 8, columns, 128),
            vmem(2, 16, 5, 8, 128),
            vmem(512, 896),
            vmem(512, 512),
            vmem(8, 3, 64, 128),
            vmem(comps, columns, cells),
            vmem(3, 3, BANDS, cells),
            vmem(1, cells),
            vmem(3, cells),
            vmem(comps, columns, 128),
            vmem(comps, columns, 128),
            vmem(3, 3, BANDS, 128),
            vmem(3, 3, BANDS, 128),
            vmem(1, 128),
            vmem(1, 128),
            vmem(3, 128),
            vmem(3, 128),
            vmem(tiles + 1, 9 * BANDS + 3, 8, 128),
            vmem(tiles, comps, columns, 128),
            vmem(2, 16, 5, 8, 128),
            vmem(16, 5, 8, 128),
            vmem(16, 5, 8, 128),
            vmem(16, 5, 8, 128),
            vmem(5, 8, 128),
            vmem(4, 5, 8, 128),
            vmem(5, 8, 128),
            vmem(4, 5, 8, 128),
            vmem(5, 8, 128),
        ]
        + [dma(8)] * 4
        + [dma(16)] * 4
        + [dma(4)] * 4
        + [dma(16)] * 4
        + [dma(5), dma(8), dma(8)],
        compiler_params=pltpu.CompilerParams(
            collective_id=0, has_side_effects=True, vmem_limit_bytes=61 * 1024 * 1024
        ),
        name="everything",
    )(offsets, probes, coupling, viscosity, weight)


def place_kernel(basis, r_rows, basis_out, r_out):
    basis_out[...] = basis[...]
    r_out[...] = r_rows[...]


def placed(basis, r_rows):
    return pl.pallas_call(
        place_kernel,
        out_shape=(struct(*basis.shape), struct(*r_rows.shape)),
        in_specs=[VMEM, VMEM],
        out_specs=(VMEM, VMEM),
        compiler_params=pltpu.CompilerParams(vmem_limit_bytes=63 * 1024 * 1024),
        name="placed",
    )(basis, r_rows)


def body(probes, viscosity, coupling, misfit_weight, band_offsets):
    return placed(
        *everything(
            band_offsets, probes, coupling.transpose(1, 2, 0, 3), viscosity[None, :], misfit_weight
        )
    )


def solution(mesh):
    return jax.shard_map(
        body,
        mesh=mesh,
        in_specs=(
            P(None, "probe", "slab"),
            P("slab"),
            P(None, None, None, "slab"),
            P(None, "slab"),
            P(),
        ),
        out_specs=(P(None, "probe", "slab"), P("probe", None)),
        check_vma=False,
    )
```
